32 devices in a mesh: section: 4 (over x, core), wide: 2 (over y), narrow: 4 (over z).
Axes of the slice: x: 2, y: 2, z: 4, core: 2. Of those that a mesh axis runs over, the one named last changes fastest.
Arguments:
- valence_orbitals: float32 [8, 48, 2304], P(None, 'narrow'), may hold values from -6 to 6
- conduction_orbitals: float32 [8, 48, 2304], P(('section', 'wide'), 'narrow'), may hold values from -6 to 6
- valence_energy: float32 [8], replicated, may hold values from -7 to -1
- conduction_energy: float32 [8], replicated, may hold values from 1 to 7
- frequency: float32 [1], replicated, may hold values from 0.5 to 4
- pair_bands: int32 [32, 2], P(('section', 'wide')), may hold values from 0 to 7, as said below
- gvec_index: int32 [12288], replicated, may hold values from 0 to 110591, as said below
Outputs:
- chi: float32 [12288, 12288], P(('section', 'narrow'), 'wide')
The draws below stay inside these ranges and needn't reach their ends.
Inputs may be any that keep to these rules, and one draw needn't show every extreme that they name: `pair_bands`: column 0 is a valence band, column 1 a conduction band; rows b * 4 to (b + 1) * 4 - 1 pair conduction band b with 4 distinct valence bands. `gvec_index`: the 12288 indices are distinct.
All inputs are finite; a program needn't handle non-finite values.
Results may differ from the reference program's by a relative error of at most 0.000094.
Values sent between devices are 32-bit elements; how exact they have to be, the bound alone decides.
No kernel may reach another device: no remote copies, remote signals or barrier semaphores. Data moves between devices by JAX's collectives and lax.ppermute only.
A program may use at most 192 MiB of HBM per device.

```python
import math
import jax
import jax.numpy as jnp
from jax import lax

GRID = 48
NG = 12288
NV = 8
PV = 4
NC = 8
PAIRS = 32
N_SECTION = 4
N_WIDE = 2


def draw_gvec_index(key, part):
    order = jax.random.permutation(jax.random.fold_in(key, 17), GRID * GRID * GRID)
    return order[:NG].astype(jnp.int32)


def draw_pair_bands(key, part):
    band_keys = jax.random.split(jax.random.fold_in(key, 29), NC)
    valence_part = jax.vmap(lambda one_key: jax.random.permutation(one_key, NV)[:PV])(band_keys).astype(jnp.int32)
    conduction_part = jnp.broadcast_to(jnp.arange(NC, dtype=jnp.int32)[:, None], (NC, PV))
    return jnp.stack([valence_part, conduction_part], axis=2).reshape(NC * PV, 2)


def block_scale(key, extent, cuts, smallest, high):
    level, own = 1.0, jax.random.fold_in(key, 6)
    for dim, shards_of in cuts:
        steps = jnp.exp(jax.random.uniform(jax.random.fold_in(own, dim), (shards_of,), jnp.float32, smallest / len(cuts), high / len(cuts)))
        level = level * jnp.repeat(steps, extent[dim] // shards_of).reshape([-1 if axis == dim else 1 for axis in range(len(extent))])
    return level


def gaussian(rng, extent, scale, reach, pieces=(), held_as=jnp.bfloat16):
    drawn = jax.random.normal(rng, extent, jnp.float32) * scale
    if len(pieces) > 0:
        drawn = block_scale(rng, extent, pieces, -0.22, 0.18) * drawn
    return jnp.clip(drawn, min=-reach, max=reach).astype(held_as)


def setup_inputs(seed: int = 0) -> dict:
    arg_keys = jax.random.split(jax.random.key(seed), 8)
    return {
        "valence_orbitals": gaussian(arg_keys[0], (NV, GRID, GRID * GRID), 1.0, 6.0, ((1, 4),), jnp.float32),
        "conduction_orbitals": gaussian(arg_keys[1], (NC, GRID, GRID * GRID), 1.0, 6.0, ((0, 8), (1, 4)), jnp.float32),
        "valence_energy": jnp.clip(jax.random.uniform(arg_keys[2], (NV,), jnp.float32, -7.0, -1.0), -7.0, -1.0),
        "conduction_energy": jnp.clip(jax.random.uniform(arg_keys[3], (NC,), jnp.float32, 1.0, 7.0), 1.0, 7.0),
        "frequency": jnp.clip(jax.random.uniform(arg_keys[4], (1,), jnp.float32, 0.5, 4.0), 0.5, 4.0),
        "pair_bands": draw_pair_bands(jax.random.fold_in(arg_keys[7], 71), 0),
        "gvec_index": draw_gvec_index(jax.random.fold_in(arg_keys[7], 71), 0),
    }


def build_cosine(length):
    wavenumber = jnp.arange(length, dtype=jnp.float32)[:, None]
    position = jnp.arange(length, dtype=jnp.float32)[None, :]
    cosine = math.sqrt(2.0 / length) * jnp.cos(math.pi * (2.0 * position + 1.0) * wavenumber / (2.0 * length))
    return jnp.where(wavenumber == 0.0, cosine * math.sqrt(0.5), cosine)

def reference(valence_orbitals, conduction_orbitals, valence_energy, conduction_energy, frequency, pair_bands, gvec_index):
    cosine = build_cosine(GRID)
    highest = lax.Precision.HIGHEST

    def one_block(band_pairs):
        valence_pick = valence_orbitals[band_pairs[:, 0]].reshape(-1, GRID, GRID, GRID)
        conduction_pick = conduction_orbitals[band_pairs[:, 1]].reshape(-1, GRID, GRID, GRID)
        density = valence_pick * conduction_pick
        sweep_one = jnp.einsum('pxyz,kz->pxyk', density, cosine, precision=highest)
        sweep_two = jnp.einsum('pxyk,jy->pxjk', sweep_one, cosine, precision=highest)
        sweep_three = jnp.einsum('pxjk,ix->pijk', sweep_two, cosine, precision=highest)
        return sweep_three.reshape(sweep_three.shape[0], -1)[:, gvec_index]
    blocks = pair_bands.reshape(N_SECTION * N_WIDE, PV, 2)
    coefficients = lax.map(one_block, blocks).reshape(PAIRS, NG)
    energy_gap = conduction_energy[pair_bands[:, 1]] - valence_energy[pair_bands[:, 0]]
    weight = -4.0 * energy_gap / (energy_gap * energy_gap + frequency[0] * frequency[0]) / math.sqrt(PAIRS)
    weighted = coefficients * weight[:, None]
    return lax.dot_general(weighted, coefficients, (((0,), (0,)), ((), ())), precision=highest, preferred_element_type=jnp.float32)
```

```python
import functools
import math

import jax
import jax.numpy as jnp
import numpy as np
from jax import lax
from jax.experimental import pallas as pl
from jax.experimental.pallas import tpu as pltpu
from jax.sharding import PartitionSpec as P

LANES = 128
ROWS = 8
F32 = jnp.float32
BF16 = jnp.bfloat16


def cosine_table(length):
    wavenumber = np.arange(length, dtype=np.float64)[:, None]
    position = np.arange(length, dtype=np.float64)[None, :]
    table = math.sqrt(2.0 / length) * np.cos(
        math.pi * (2.0 * position + 1.0) * wavenumber / (2.0 * length)
    )
    table[0] *= math.sqrt(0.5)
    return table.astype(np.float32)


def split(value):
    high = value.astype(BF16)
    low = (value - high.astype(F32)).astype(BF16)
    return high, low


def z_weights(cosine, per_chunk, slot):
    extent = cosine.shape[0]
    out = np.zeros((per_chunk * extent, per_chunk * slot), np.float32)
    for y in range(per_chunk):
        out[y * extent : (y + 1) * extent, y * slot : y * slot + extent] = cosine.T
    return out


def y_weights(cosine):
    extent = cosine.shape[0]
    half = cosine[:, : extent // 2].reshape(extent * extent // 4, 2)
    return np.repeat(half, LANES // 2, axis=1)


def x_tables(cosine, planes, pairs):
    extent = cosine.shape[0]
    out = np.zeros((extent // planes, planes * pairs, LANES), np.float32)
    for part in range(extent // planes):
        block = cosine[:, part * planes : (part + 1) * planes].T
        out[part, :, :extent] = np.repeat(block, pairs, axis=0)
    return out


def pick_blocks(extent, rows, pairs, count, block_of, index_ref, table_ref, scaled_ref, out_ref, lane_ref, chunk_ref, first_ref, basis_ref):
    tiles = rows // ROWS
    per_plane = extent * extent // LANES
    index = index_ref[...]
    lane_ref[...] = index & (LANES - 1)
    upper = index >> (LANES.bit_length() - 1)
    plane = (upper * ((1 << 16) // per_plane + 1)) >> 16
    first_ref[...] = plane
    chunk_ref[...] = upper - plane * per_plane
    for s in range(per_plane):
        high, low = split(table_ref[s])
        basis_ref[pl.ds(0, rows), pl.ds(s * LANES, LANES)] = high
        basis_ref[pl.ds(rows, rows), pl.ds(s * LANES, LANES)] = low
    take = functools.partial(jnp.take_along_axis, axis=1, mode="promise_in_bounds")
    wide = 2 * LANES
    steps = extent * extent // wide
    inside = lax.broadcasted_iota(jnp.int32, (wide, wide), 0).astype(F32).astype(BF16)
    one = jnp.ones((), BF16)
    zero = jnp.zeros((), BF16)

    def row_of(ref, b):
        return jnp.broadcast_to(ref[pl.ds(b, 1), :], (ROWS, LANES))

    def finish(q, b, picked):
        first = row_of(first_ref, b)
        out = None
        for t in range(tiles):
            term = picked[t] * take(scaled_ref[pl.ds(t * ROWS, ROWS), :], first)
            out = term if out is None else out + term
        out = out + pltpu.roll(out, pairs, 0)
        out_ref[q] = out[:pairs]

    def three(step, carry):
        places = [step * 3 + u for u in range(3)]
        ids = [block_of(q) for q in places]
        lane = jnp.concatenate([lane_ref[pl.ds(b, 1), :] for b in ids[:2]], axis=1)
        chunk = jnp.concatenate([chunk_ref[pl.ds(b, 1), :] for b in ids[:2]], axis=1)
        within = lane + (chunk & 1) * LANES
        tile = chunk >> 1
        total = jnp.zeros((2 * rows, wide), F32)
        third_lane, third_chunk = row_of(lane_ref, ids[2]), row_of(chunk_ref, ids[2])
        third = [None] * tiles
        for s in range(steps):
            key = jnp.where(tile == s, within, -1).astype(F32).astype(BF16)
            hot = jnp.where(inside == key, one, zero)
            total = total + jnp.dot(basis_ref[:, pl.ds(s * wide, wide)], hot, preferred_element_type=F32)
            for c in (2 * s, 2 * s + 1):
                for t in range(tiles):
                    found = take(table_ref[c, pl.ds(t * ROWS, ROWS), :], third_lane)
                    third[t] = found if c == 0 else jnp.where(third_chunk == c, found, third[t])
        picked = total[:rows] + total[rows:]
        for u in range(2):
            finish(places[u], ids[u], [picked[t * ROWS : (t + 1) * ROWS, u * LANES : (u + 1) * LANES] for t in range(tiles)])
        finish(places[2], ids[2], third)
        return carry

    lax.fori_loop(0, count // 3, three, 0, unroll=4)


def sweep_kernel(
    sizes,
    bands_ref,
    valence_energy_ref,
    conduction_energy_ref,
    frequency_ref,
    valence_ref,
    conduction_ref,
    z_high_ref,
    z_low_ref,
    y_ref,
    x_ref,
    index_ref,
    out_ref,
    table_ref,
    scaled_ref,
    density_ref,
    fold_ref,
    lane_ref,
    chunk_ref,
    first_ref,
    basis_ref,
):
    extent, planes, pairs, total_pairs, count, block_of = sizes
    rows = planes * pairs
    tiles = rows // ROWS
    per_chunk = 3 * LANES // extent
    groups = extent // per_chunk
    narrow_pos = lax.axis_index("narrow")
    band_offset = (lax.axis_index("section") * lax.axis_size("wide") + lax.axis_index("wide")) * conduction_ref.shape[0]
    for p in range(pairs):
        v = bands_ref[p, 0]
        c = bands_ref[p, 1] - band_offset
        for m in range(groups):
            for part in range(3):
                lanes = pl.ds((m * 3 + part) * LANES, LANES)
                density_ref[m, part, pl.ds(p, planes, stride=pairs), :] = valence_ref[v, :, lanes] * conduction_ref[c, :, lanes]
    density = jnp.concatenate([density_ref[:, part].reshape(groups * rows, LANES) for part in range(3)], axis=1)
    high, low = split(density)
    dot = functools.partial(jnp.dot, preferred_element_type=F32)
    swept = dot(high, z_high_ref[...]) + dot(low, z_high_ref[...]) + dot(high, z_low_ref[...])
    quarter = per_chunk // 2
    for m in range(groups // 2):
        for q in range(quarter):
            near = swept[m * rows : (m + 1) * rows, q * LANES : (q + 1) * LANES]
            far_m, far_q = groups - 1 - m, quarter - 1 - q
            far = swept[far_m * rows : (far_m + 1) * rows, far_q * LANES : (far_q + 1) * LANES]
            far = pltpu.roll(far, LANES // 2, 1)
            fold_ref[0, m * quarter + q] = near + far
            fold_ref[1, m * quarter + q] = near - far
    terms = extent // 4
    lane_id = lax.broadcasted_iota(jnp.int32, (ROWS, LANES), 1)

    def sweep_tile(t, carry):
        where_rows = pl.ds(pl.multiple_of(t * ROWS, ROWS), ROWS)
        parts = [[fold_ref[par, s, where_rows, :] for s in range(terms)] for par in range(2)]
        chunks = {}
        for j in range(extent):
            total = None
            for s in range(terms):
                term = parts[j % 2][s] * y_ref[pl.ds(j * terms + s, 1), :]
                total = term if total is None else total + term
            total = total + pltpu.roll(total, LANES // 2, 1)
            start = j * extent
            offset = start % LANES
            moved = total if offset % (LANES // 2) == 0 else pltpu.roll(total, offset, 1)
            for chunk in range(start // LANES, (start + extent - 1) // LANES + 1):
                begin = start - chunk * LANES
                chunks[chunk] = moved if begin <= 0 else jnp.where(lane_id >= begin, moved, chunks[chunk])
                if start + extent >= (chunk + 1) * LANES:
                    table_ref[chunk, where_rows, :] = chunks.pop(chunk)
        return carry

    lax.fori_loop(0, tiles, sweep_tile, 0)
    row_pair = lax.broadcasted_iota(jnp.int32, (ROWS, LANES), 0) % pairs
    gap = jnp.zeros((ROWS, LANES), F32)
    for p in range(pairs):
        one_gap = conduction_energy_ref[bands_ref[p, 1]] - valence_energy_ref[bands_ref[p, 0]]
        gap = jnp.where(row_pair == p, one_gap, gap)
    frequency = frequency_ref[0]
    scale = jnp.sqrt(4.0 * gap / (gap * gap + frequency * frequency) / math.sqrt(total_pairs))
    for t in range(tiles):
        scaled_ref[pl.ds(t * ROWS, ROWS), :] = x_ref[narrow_pos, pl.ds(t * ROWS, ROWS), :] * scale
    pick_blocks(extent, rows, pairs, count, block_of(), index_ref, table_ref, scaled_ref, out_ref, lane_ref, chunk_ref, first_ref, basis_ref)


def pick_kernel(sizes, index_ref, table_ref, scaled_ref, out_ref, lane_ref, chunk_ref, first_ref, basis_ref):
    extent, rows, pairs, count, block_of = sizes
    pick_blocks(extent, rows, pairs, count, block_of(), index_ref, table_ref, scaled_ref, out_ref, lane_ref, chunk_ref, first_ref, basis_ref)


def whole(shape):
    return pl.BlockSpec(shape, lambda i: (0,) * len(shape))


SMEM = pl.BlockSpec(memory_space=pltpu.SMEM)


def pick_scratch(blocks, rows, area):
    return [pltpu.VMEM((blocks, LANES), jnp.int32)] * 3 + [pltpu.VMEM((2 * rows, area), BF16)]


def sweep_call(bands, valence_energy, conduction_energy, frequency, valence, conduction, index, total_pairs, count, block_of):
    pairs = bands.shape[0]
    planes, area = valence.shape[1], valence.shape[2]
    extent = math.isqrt(area)
    rows = planes * pairs
    cosine = cosine_table(extent)
    per_chunk = 3 * LANES // extent
    groups = extent // per_chunk
    weights = z_weights(cosine, per_chunk, LANES // 2)
    z_high = weights.astype(BF16)
    z_low = (weights - z_high.astype(np.float32)).astype(BF16)
    operands = [valence, conduction, jnp.asarray(z_high), jnp.asarray(z_low)]
    operands += [jnp.asarray(y_weights(cosine)), jnp.asarray(x_tables(cosine, planes, pairs)), index]
    shapes = [(count, pairs, LANES), (area // LANES, rows, LANES), (rows, LANES)]
    return pl.pallas_call(
        functools.partial(sweep_kernel, (extent, planes, pairs, total_pairs, count, block_of)),
        grid=(1,),
        out_shape=[jax.ShapeDtypeStruct(shape, F32) for shape in shapes],
        in_specs=[SMEM] * 4 + [whole(a.shape) for a in operands],
        out_specs=[whole(shape) for shape in shapes],
        scratch_shapes=[
            pltpu.VMEM((groups, 3, rows, LANES), F32),
            pltpu.VMEM((2, extent // 4, rows, LANES), F32),
        ]
        + pick_scratch(index.shape[0], rows, area),
        cost_estimate=pl.CostEstimate(flops=8_000_000_000, bytes_accessed=4_000_000, transcendentals=0),
        name="sweep",
    )(bands, valence_energy, conduction_energy, frequency, *operands)


def pick_call(index, table, scaled, pairs, count, block_of):
    rows = table.shape[1]
    area = table.shape[0] * LANES
    return pl.pallas_call(
        functools.partial(pick_kernel, (math.isqrt(area), rows, pairs, count, block_of)),
        grid=(1,),
        out_shape=jax.ShapeDtypeStruct((count, pairs, LANES), F32),
        in_specs=[whole(a.shape) for a in (index, table, scaled)],
        out_specs=whole((count, pairs, LANES)),
        scratch_shapes=pick_scratch(index.shape[0], rows, area),
        cost_estimate=pl.CostEstimate(flops=4_000_000_000, bytes_accessed=1_000_000, transcendentals=0),
        name="pick",
    )(index, table, scaled)


def arrange_kernel(row_tiles, near_ref, far_ref, own_ref, wide_ref, narrow_ref, both_ref):
    narrow_count = lax.axis_size("narrow")
    half = narrow_count * row_tiles
    wide_pos, narrow_pos = lax.axis_index("wide"), lax.axis_index("narrow")
    for out_ref, w, n in (
        (own_ref, wide_pos, narrow_pos),
        (wide_ref, 1 - wide_pos, narrow_pos),
        (narrow_ref, wide_pos, narrow_pos ^ 1),
        (both_ref, 1 - wide_pos, narrow_pos ^ 1),
    ):
        columns = pl.ds(w * half, half)
        rows = pl.ds((1 - w) * half + n * row_tiles, row_tiles)
        out_ref[pl.ds(0, half)] = near_ref[columns] + far_ref[columns]
        out_ref[pl.ds(half, row_tiles)] = near_ref[rows] + far_ref[rows]


def arrange_call(near, far, row_tiles):
    blocks, pairs, _ = near.shape
    shape = (blocks // 2 + row_tiles, pairs, LANES)
    return pl.pallas_call(
        functools.partial(arrange_kernel, row_tiles),
        grid=(1,),
        out_shape=[jax.ShapeDtypeStruct(shape, F32)] * 4,
        in_specs=[whole(near.shape)] * 2,
        out_specs=[whole(shape)] * 4,
        name="arrange",
    )(near, far)


def stack_split(value, order):
    high, low = split(value)
    return jnp.concatenate([low if part else high for part in order], axis=0)


def product_kernel(row_tiles, pairs, own_ref, across_ref, core_ref, far_ref, out_ref, rows_ref, gather_ref):
    section, wide_pos, narrow_pos = lax.axis_index("section"), lax.axis_index("wide"), lax.axis_index("narrow")
    parity = narrow_pos & 1
    narrow_count = lax.axis_size("narrow")
    half = narrow_count * row_tiles
    sources = (own_ref, across_ref, core_ref, far_ref)

    def collect(kind, start):
        for i, ref in enumerate(sources):
            for b in range(2):
                rows = pl.ds((2 * i + b) * pairs, pairs)
                for r in range(row_tiles):
                    gather_ref[rows, pl.ds(r * LANES, LANES)] = ref[2 * kind + b, start + r]
        return gather_ref[...]

    step = pl.program_id(0)

    @pl.when(step == 0)
    def _():
        start = jnp.where(section // 2 == wide_pos, narrow_pos * row_tiles, half)
        value = collect((section & 1) ^ parity, start)
        high, low = split(-value)
        high, low = high.astype(F32), low.astype(F32)
        stacked = jnp.concatenate([high, high, low, low], axis=0)
        rows_ref[...] = stacked.T.astype(BF16)

    value = collect((step // narrow_count) ^ parity, (step % narrow_count) * row_tiles)
    out_ref[...] = jnp.dot(rows_ref[...], stack_split(value, (0, 1, 0, 1)), preferred_element_type=F32)


def product_call(sources, row_tiles):
    _, blocks, pairs, _ = sources[0].shape
    row_block = row_tiles * LANES
    narrow_count = blocks // row_tiles - 1
    depth = 2 * len(sources) * pairs
    return pl.pallas_call(
        functools.partial(product_kernel, row_tiles, pairs),
        grid=(2 * narrow_count,),
        out_shape=jax.ShapeDtypeStruct((row_block, 2 * narrow_count * row_block), F32),
        in_specs=[whole(a.shape) for a in sources],
        out_specs=pl.BlockSpec((row_block, row_block), lambda i: (0, i)),
        scratch_shapes=[pltpu.VMEM((row_block, 4 * depth), BF16), pltpu.VMEM((depth, row_block), F32)],
        name="product",
    )(*sources)


def contract(left_rows, right_rows):
    return lax.dot_general(
        left_rows,
        right_rows,
        (((0,), (0,)), ((), ())),
        precision=lax.Precision.HIGHEST,
        preferred_element_type=F32,
    )


def on_device(valence, conduction, valence_energy, conduction_energy, frequency, pair_bands, gvec_index):
    pairs = pair_bands.shape[0]
    section_count, wide_count, narrow_count = (lax.axis_size(name) for name in ("section", "wide", "narrow"))
    total_pairs = pairs * section_count * wide_count
    vector_count = gvec_index.shape[0]
    row_block = vector_count // (section_count * narrow_count)
    column_block = vector_count // wide_count
    row_tiles = row_block // LANES
    blocks = vector_count // LANES
    index = gvec_index.reshape(blocks, LANES)
    sweep = functools.partial(sweep_call, pair_bands, valence_energy, conduction_energy, frequency, valence, conduction, index, total_pairs)

    if not (section_count == 4 and wide_count == 2 and narrow_count == 4):
        partial_value = sweep(blocks, lambda: lambda q: q)[0]
        partial_value = jnp.swapaxes(partial_value, 0, 1).reshape(pairs, section_count, narrow_count, row_block)
        own_rows = lax.psum_scatter(partial_value, "narrow", scatter_dimension=2, tiled=True)
        coefficients = lax.all_gather(own_rows, "narrow", axis=2, tiled=True).reshape(pairs, vector_count)
        row_send = own_rows.reshape(pairs, section_count, row_block)
        row_recv = lax.all_to_all(row_send, "section", split_axis=1, concat_axis=0, tiled=True)
        row_recv = row_recv.reshape(section_count, pairs, row_block)
        column_send = coefficients.reshape(pairs, wide_count, column_block)
        column_recv = lax.all_to_all(column_send, "wide", split_axis=1, concat_axis=0, tiled=True)
        column_recv = column_recv.reshape(wide_count * pairs, column_block)
        rows_all = lax.all_gather(row_recv, "wide", axis=1, tiled=True).reshape(-1, row_block)
        return contract(-rows_all, lax.all_gather(column_recv, "section", axis=0, tiled=True))

    half = narrow_count * row_tiles

    def block_of(other):
        def make():
            own = (lax.axis_index("narrow") & 1) ^ other
            return lambda q: q + (q // half + own) * half

        return make

    away, table, scaled = sweep(blocks // 2, block_of(1))
    kept = pick_call(index, table, scaled, pairs, blocks // 2, block_of(0))
    flip = lambda bit: [(i, i ^ bit) for i in range(4)]
    summed = kept + lax.ppermute(away, "narrow", flip(1))
    opposite = lax.ppermute(summed, "narrow", flip(2))
    own, to_wide, to_narrow, to_both = arrange_call(summed, opposite, row_tiles)
    from_wide = lax.ppermute(to_wide, "wide", [(0, 1), (1, 0)])
    from_narrow = lax.ppermute(to_narrow, "narrow", flip(1))
    from_both = lax.ppermute(to_both, ("wide", "narrow"), [(i, i ^ 5) for i in range(8)])
    near = jnp.stack([own, from_wide, from_narrow, from_both])
    across = lax.ppermute(near, "section", flip(2))
    core = lax.ppermute(near, "section", flip(1))
    far = lax.ppermute(across, "section", flip(1))
    return product_call((near, across, core, far), row_tiles)


def solution(mesh):
    in_specs = (
        P(None, "narrow", None),
        P(("section", "wide"), "narrow", None),
        P(),
        P(),
        P(),
        P(("section", "wide"), None),
        P(),
    )
    out_specs = P(("section", "narrow"), "wide")
    return jax.shard_map(on_device, mesh=mesh, in_specs=in_specs, out_specs=out_specs, check_vma=False)
```

```python
import functools
import math

import jax
import jax.numpy as jnp
import numpy as np
from jax import lax
from jax.experimental import pallas as pl
from jax.experimental.pallas import tpu as pltpu
from jax.sharding import PartitionSpec as P

LANES = 128
ROWS = 8
F32 = jnp.float32
BF16 = jnp.bfloat16


def cosine_table(length):
    wavenumber = np.arange(length, dtype=np.float64)[:, None]
    position = np.arange(length, dtype=np.float64)[None, :]
    table = math.sqrt(2.0 / length) * np.cos(
        math.pi * (2.0 * position + 1.0) * wavenumber / (2.0 * length)
    )
    table[0] *= math.sqrt(0.5)
    return table.astype(np.float32)


def split(value):
    high = value.astype(BF16)
    low = (value - high.astype(F32)).astype(BF16)
    return high, low


def z_weights(cosine, per_chunk, slot):
    extent = cosine.shape[0]
    out = np.zeros((per_chunk * extent, per_chunk * slot), np.float32)
    for y in range(per_chunk):
        out[y * extent : (y + 1) * extent, y * slot : y * slot + extent] = cosine.T
    return out


def y_weights(cosine):
    extent = cosine.shape[0]
    half = cosine[:, : extent // 2].reshape(extent * extent // 4, 2)
    return np.repeat(half, LANES // 2, axis=1)


def x_tables(cosine, planes, pairs):
    extent = cosine.shape[0]
    out = np.zeros((extent // planes, planes * pairs, LANES), np.float32)
    for part in range(extent // planes):
        block = cosine[:, part * planes : (part + 1) * planes].T
        out[part, :, :extent] = np.repeat(block, pairs, axis=0)
    return out


def pick_blocks(pairs, count, block_of, index_ref, table_ref, scaled_ref, out_ref, basis_ref, lane_ref, chunk_ref, first_ref):
    per_plane, rows, _ = table_ref.shape
    tiles = rows // ROWS
    for s in range(per_plane):
        high, low = split(table_ref[s])
        basis_ref[pl.ds(s * rows, rows), pl.ds(0, LANES)] = high
        basis_ref[pl.ds(s * rows, rows), pl.ds(LANES, LANES)] = low
    index = index_ref[...]
    lane_ref[...] = index & (LANES - 1)
    upper = index >> (LANES.bit_length() - 1)
    plane = (upper * ((1 << 16) // per_plane + 1)) >> 16
    first_ref[...] = plane
    chunk_ref[...] = upper - plane * per_plane
    take = functools.partial(jnp.take_along_axis, axis=1, mode="promise_in_bounds")
    wide = 2 * LANES
    inside = lax.broadcasted_iota(jnp.int32, (LANES, wide), 0).astype(F32).astype(BF16)
    one = jnp.ones((), BF16)
    zero = jnp.zeros((), BF16)

    def row_of(ref, b):
        return jnp.broadcast_to(ref[pl.ds(b, 1), :], (ROWS, LANES))

    def select(chunk, candidate):
        picked = [None] * tiles
        for c in range(per_plane):
            mine = chunk == c
            for t in range(tiles):
                found = candidate(c, t)
                picked[t] = found if c == 0 else jnp.where(mine, found, picked[t])
        return picked

    def finish(q, b, picked):
        first = row_of(first_ref, b)
        out = None
        for t in range(tiles):
            term = picked[t] * take(scaled_ref[pl.ds(t * ROWS, ROWS), :], first)
            out = term if out is None else out + term
        out = out + pltpu.roll(out, pairs, 0)
        out_ref[q] = out[:pairs]

    def three(step, carry):
        places = [step * 3 + u for u in range(3)]
        ids = [block_of(q) for q in places]
        lane = jnp.concatenate([lane_ref[pl.ds(b, 1), :] for b in ids[:2]], axis=1)
        hot = jnp.where(inside == lane.astype(F32).astype(BF16), one, zero)
        offers = jnp.dot(basis_ref[...], jnp.concatenate([hot, hot], axis=0), preferred_element_type=F32)
        third_lane = row_of(lane_ref, ids[2])
        third = select(row_of(chunk_ref, ids[2]), lambda c, t: take(table_ref[c, pl.ds(t * ROWS, ROWS), :], third_lane))
        chunk = jnp.concatenate([row_of(chunk_ref, b) for b in ids[:2]], axis=1)
        picked = select(chunk, lambda c, t: offers[c * rows + t * ROWS : c * rows + (t + 1) * ROWS])
        for u in range(2):
            finish(places[u], ids[u], [value[:, u * LANES : (u + 1) * LANES] for value in picked])
        finish(places[2], ids[2], third)
        return carry

    lax.fori_loop(0, count // 3, three, 0, unroll=4)


def sweep_kernel(
    sizes,
    bands_ref,
    valence_energy_ref,
    conduction_energy_ref,
    frequency_ref,
    *refs,
):
    given, (out_ref, *kept), held = refs[:7], refs[7:10], refs[10:17]
    table_ref, scaled_ref, density_ref, fold_ref, *picking, sems, store_sems = refs[17:]
    stores = [pltpu.make_async_copy(source, target, store_sems.at[i]) for i, (source, target) in enumerate(zip((table_ref, scaled_ref), kept))]
    loads = [pltpu.make_async_copy(source, target, sems.at[i]) for i, (source, target) in enumerate(zip(given, held))]
    for load in loads:
        load.start()
    valence_ref, conduction_ref, z_high_ref, z_low_ref, y_ref, x_ref, index_ref = held
    extent, planes, pairs, total_pairs, count, block_of = sizes
    rows = planes * pairs
    tiles = rows // ROWS
    per_tile = ROWS // pairs
    per_chunk = 3 * LANES // extent
    groups = extent // per_chunk
    row_id = lax.broadcasted_iota(jnp.int32, (ROWS, LANES), 0)
    lane_id = lax.broadcasted_iota(jnp.int32, (ROWS, LANES), 1)
    band = jnp.zeros((ROWS, LANES), jnp.int32)
    for p in range(pairs):
        band = jnp.where(row_id % pairs == p, bands_ref[0, p], band)
    loads[0].wait()
    loads[1].wait()
    for m in range(groups):
        for part in range(3):
            lanes = pl.ds((m * 3 + part) * LANES, LANES)
            for t in range(tiles):
                value, factor = None, None
                for u in range(per_tile):
                    plane = t * per_tile + u
                    picked = jnp.take_along_axis(valence_ref[plane, :, lanes], band, axis=0, mode="promise_in_bounds")
                    other = jnp.broadcast_to(conduction_ref[plane, :, lanes], (ROWS, LANES))
                    value = picked if u == 0 else jnp.where(row_id >= u * pairs, picked, value)
                    factor = other if u == 0 else jnp.where(row_id >= u * pairs, other, factor)
                density_ref[part, pl.ds(m * rows + t * ROWS, ROWS), :] = value * factor
    density = jnp.concatenate([density_ref[part] for part in range(3)], axis=1)
    high, low = split(density)
    loads[2].wait()
    loads[3].wait()
    dot = functools.partial(jnp.dot, preferred_element_type=F32)
    swept = dot(high, z_high_ref[...]) + dot(low, z_high_ref[...]) + dot(high, z_low_ref[...])
    quarter = per_chunk // 2
    for m in range(groups // 2):
        for q in range(quarter):
            near = swept[m * rows : (m + 1) * rows, q * LANES : (q + 1) * LANES]
            far_m, far_q = groups - 1 - m, quarter - 1 - q
            far = swept[far_m * rows : (far_m + 1) * rows, far_q * LANES : (far_q + 1) * LANES]
            far = pltpu.roll(far, LANES // 2, 1)
            fold_ref[0, m * quarter + q] = near + far
            fold_ref[1, m * quarter + q] = near - far
    terms = extent // 4
    block = 2 * ROWS
    loads[4].wait()

    def sweep_tiles(t, carry):
        where_rows = pl.ds(pl.multiple_of(t * block, block), block)
        for parity in range(2):
            parts = [fold_ref[parity, s, where_rows, :] for s in range(terms)]
            for j in range(parity, extent, 2):
                total = None
                for s in range(terms):
                    term = parts[s] * y_ref[pl.ds(j * terms + s, 1), :]
                    total = term if total is None else total + term
                total = total + pltpu.roll(total, LANES // 2, 1)
                start = j * extent
                offset = start % LANES
                moved = total if offset % (LANES // 2) == 0 else pltpu.roll(total, offset, 1)
                for chunk in range(start // LANES, (start + extent - 1) // LANES + 1):
                    low_lane = max(start - chunk * LANES, 0)
                    high_lane = min(start + extent - chunk * LANES, LANES)
                    table_ref[chunk, where_rows, low_lane:high_lane] = moved[:, low_lane:high_lane]
        return carry

    lax.fori_loop(0, rows // block, sweep_tiles, 0)
    loads[5].wait()
    loads[6].wait()
    narrow_pos = lax.axis_index("narrow")
    gap = jnp.zeros((ROWS, LANES), F32)
    for p in range(pairs):
        one_gap = conduction_energy_ref[bands_ref[1, p]] - valence_energy_ref[bands_ref[0, p]]
        gap = jnp.where(row_id % pairs == p, one_gap, gap)
    frequency = frequency_ref[0]
    scale = jnp.sqrt(4.0 * gap / (gap * gap + frequency * frequency) / math.sqrt(total_pairs))
    for t in range(tiles):
        scaled_ref[pl.ds(t * ROWS, ROWS), :] = x_ref[narrow_pos, pl.ds(t * ROWS, ROWS), :] * scale
    for store in stores:
        store.start()
    pick_blocks(pairs, count, block_of(), index_ref, table_ref, scaled_ref, out_ref, *picking)
    for store in stores:
        store.wait()


def pick_kernel(pairs, count, block_of, *refs):
    given, out_ref, held, picking, sems = refs[:3], refs[3], refs[4:7], refs[7:11], refs[11]
    loads = [pltpu.make_async_copy(source, target, sems.at[i]) for i, (source, target) in enumerate(zip(given, held))]
    for load in loads:
        load.start()
    for load in loads:
        load.wait()
    pick_blocks(pairs, count, block_of(), *held, out_ref, *picking)


def pick_scratch(index, table):
    blocks, (chunks, rows, _) = index.shape[0], table.shape
    return [pltpu.VMEM((chunks * rows, 2 * LANES), BF16)] + [pltpu.VMEM((blocks, LANES), jnp.int32)] * 3


SMEM = pl.BlockSpec(memory_space=pltpu.SMEM)
VMEM = pl.BlockSpec(memory_space=pltpu.VMEM)
HBM = pl.BlockSpec(memory_space=pltpu.HBM)


def sweep_call(bands, valence_energy, conduction_energy, frequency, valence, conduction, index, total_pairs, count, block_of):
    pairs = bands.shape[1]
    planes, area = valence.shape[0], valence.shape[2]
    extent = math.isqrt(area)
    rows = planes * pairs
    cosine = cosine_table(extent)
    per_chunk = 3 * LANES // extent
    groups = extent // per_chunk
    weights = z_weights(cosine, per_chunk, LANES // 2)
    z_high = weights.astype(BF16)
    z_low = (weights - z_high.astype(np.float32)).astype(BF16)
    operands = [valence, conduction, jnp.asarray(z_high), jnp.asarray(z_low)]
    operands += [jnp.asarray(y_weights(cosine)), jnp.asarray(x_tables(cosine, planes, pairs)), index]
    chunks = area // LANES
    table = jax.ShapeDtypeStruct((area // LANES, rows, LANES), F32)
    scaled = jax.ShapeDtypeStruct((rows, LANES), F32)
    return pl.pallas_call(
        functools.partial(sweep_kernel, (extent, planes, pairs, total_pairs, count, block_of)),
        out_shape=[jax.ShapeDtypeStruct((count, pairs, LANES), F32), table, scaled],
        in_specs=[SMEM] * 4 + [HBM] * len(operands),
        out_specs=[VMEM, HBM, HBM],
        scratch_shapes=[pltpu.VMEM(a.shape, a.dtype) for a in operands]
        + [
            pltpu.VMEM(table.shape, F32),
            pltpu.VMEM(scaled.shape, F32),
            pltpu.VMEM((3, groups * rows, LANES), F32),
            pltpu.VMEM((2, extent // 4, rows, LANES), F32),
        ]
        + pick_scratch(index, table)
        + [pltpu.SemaphoreType.DMA((len(operands),)), pltpu.SemaphoreType.DMA((2,))],
        cost_estimate=pl.CostEstimate(flops=8_000_000_000, bytes_accessed=4_000_000, transcendentals=0),
        name="sweep",
    )(bands, valence_energy, conduction_energy, frequency, *operands)


def pick_call(index, table, scaled, pairs, count, block_of):
    operands = (index, table, scaled)
    return pl.pallas_call(
        functools.partial(pick_kernel, pairs, count, block_of),
        out_shape=jax.ShapeDtypeStruct((count, pairs, LANES), F32),
        in_specs=[HBM] * 3,
        out_specs=VMEM,
        scratch_shapes=[pltpu.VMEM(a.shape, a.dtype) for a in operands] + pick_scratch(index, table) + [pltpu.SemaphoreType.DMA((3,))],
        cost_estimate=pl.CostEstimate(flops=4_000_000_000, bytes_accessed=1_000_000, transcendentals=0),
        name="pick",
    )(*operands)


def arrange_kernel(row_tiles, near_ref, far_ref, own_ref, wide_ref, narrow_ref, both_ref):
    narrow_count = lax.axis_size("narrow")
    half = narrow_count * row_tiles
    wide_pos, narrow_pos = lax.axis_index("wide"), lax.axis_index("narrow")
    for out_ref, w, n in (
        (own_ref, wide_pos, narrow_pos),
        (wide_ref, 1 - wide_pos, narrow_pos),
        (narrow_ref, wide_pos, narrow_pos ^ 1),
        (both_ref, 1 - wide_pos, narrow_pos ^ 1),
    ):
        columns = pl.ds(w * half, half)
        rows = pl.ds((1 - w) * half + n * row_tiles, row_tiles)
        out_ref[pl.ds(0, half)] = near_ref[columns] + far_ref[columns]
        out_ref[pl.ds(half, row_tiles)] = near_ref[rows] + far_ref[rows]


def arrange_call(near, far, row_tiles):
    blocks, pairs, _ = near.shape
    shape = (blocks // 2 + row_tiles, pairs, LANES)
    return pl.pallas_call(
        functools.partial(arrange_kernel, row_tiles),
        out_shape=[jax.ShapeDtypeStruct(shape, F32)] * 4,
        in_specs=[VMEM] * 2,
        out_specs=[VMEM] * 4,
        compiler_params=pltpu.CompilerParams(vmem_limit_bytes=16 << 20),
        name="arrange",
    )(near, far)


def product_kernel(row_tiles, pairs, own_ref, across_ref, core_ref, far_ref, out_ref, rows_ref, gather_ref, value_ref, sems):
    section, wide_pos, narrow_pos = lax.axis_index("section"), lax.axis_index("wide"), lax.axis_index("narrow")
    parity = narrow_pos & 1
    narrow_count = lax.axis_size("narrow")
    half = narrow_count * row_tiles
    sources = (own_ref, across_ref, core_ref, far_ref)
    row_block = rows_ref.shape[0]

    def collect(kind, start):
        for i, ref in enumerate(sources):
            for b in range(2):
                rows = pl.ds((2 * i + b) * pairs, pairs)
                for r in range(row_tiles):
                    gather_ref[rows, pl.ds(r * LANES, LANES)] = ref[2 * kind + b, start + r]
        return gather_ref[...]

    start = jnp.where(section // 2 == wide_pos, narrow_pos * row_tiles, half)
    high, low = split(-collect((section & 1) ^ parity, start))
    high, low = high.astype(F32), low.astype(F32)
    rows_ref[...] = jnp.concatenate([high, high, low, low], axis=0).T.astype(BF16)

    def copy_of(step):
        columns = pl.ds(pl.multiple_of(step * row_block, row_block), row_block)
        return pltpu.make_async_copy(value_ref.at[:, columns], out_ref.at[:, columns], sems.at[step])

    def one_block(step, carry):
        high, low = split(collect((step // narrow_count) ^ parity, (step % narrow_count) * row_tiles))
        stacked = jnp.concatenate([high, low, high, low], axis=0)
        columns = pl.ds(pl.multiple_of(step * row_block, row_block), row_block)
        value_ref[:, columns] = jnp.dot(rows_ref[...], stacked, preferred_element_type=F32)
        copy_of(step).start()
        return carry

    def wait_block(step, carry):
        copy_of(step).wait()
        return carry

    steps = 2 * narrow_count
    lax.fori_loop(0, steps, one_block, 0)
    lax.fori_loop(0, steps, wait_block, 0)


def product_call(sources, row_tiles):
    _, blocks, pairs, _ = sources[0].shape
    row_block = row_tiles * LANES
    steps = 2 * (blocks // row_tiles - 1)
    depth = 2 * len(sources) * pairs
    return pl.pallas_call(
        functools.partial(product_kernel, row_tiles, pairs),
        out_shape=jax.ShapeDtypeStruct((row_block, steps * row_block), F32),
        in_specs=[VMEM] * len(sources),
        out_specs=pl.BlockSpec(memory_space=pl.ANY),
        scratch_shapes=[
            pltpu.VMEM((row_block, 4 * depth), BF16),
            pltpu.VMEM((depth, row_block), F32),
            pltpu.VMEM((row_block, steps * row_block), F32),
            pltpu.SemaphoreType.DMA((steps,)),
        ],
        compiler_params=pltpu.CompilerParams(vmem_limit_bytes=40 << 20),
        name="product",
    )(*sources)


def contract(left_rows, right_rows):
    return lax.dot_general(
        left_rows,
        right_rows,
        (((0,), (0,)), ((), ())),
        precision=lax.Precision.HIGHEST,
        preferred_element_type=F32,
    )


def on_device(valence, conduction, valence_energy, conduction_energy, frequency, pair_bands, gvec_index):
    pairs = pair_bands.shape[0]
    section_count, wide_count, narrow_count = (lax.axis_size(name) for name in ("section", "wide", "narrow"))
    total_pairs = pairs * section_count * wide_count
    vector_count = gvec_index.shape[0]
    row_block = vector_count // (section_count * narrow_count)
    column_block = vector_count // wide_count
    row_tiles = row_block // LANES
    blocks = vector_count // LANES
    index = gvec_index.reshape(blocks, LANES)
    valence, conduction = (jnp.swapaxes(orbitals, 0, 1) for orbitals in (valence, conduction))
    energies = (valence_energy, conduction_energy, frequency)
    sweep = functools.partial(sweep_call, pair_bands.T, *energies, valence, conduction, index, total_pairs)

    if not (section_count == 4 and wide_count == 2 and narrow_count == 4):
        partial_value = sweep(blocks, lambda: lambda q: q)[0]
        partial_value = jnp.swapaxes(partial_value, 0, 1).reshape(pairs, section_count, narrow_count, row_block)
        own_rows = lax.psum_scatter(partial_value, "narrow", scatter_dimension=2, tiled=True)
        coefficients = lax.all_gather(own_rows, "narrow", axis=2, tiled=True).reshape(pairs, vector_count)
        row_send = own_rows.reshape(pairs, section_count, row_block)
        row_recv = lax.all_to_all(row_send, "section", split_axis=1, concat_axis=0, tiled=True)
        row_recv = row_recv.reshape(section_count, pairs, row_block)
        column_send = coefficients.reshape(pairs, wide_count, column_block)
        column_recv = lax.all_to_all(column_send, "wide", split_axis=1, concat_axis=0, tiled=True)
        column_recv = column_recv.reshape(wide_count * pairs, column_block)
        rows_all = lax.all_gather(row_recv, "wide", axis=1, tiled=True).reshape(-1, row_block)
        return contract(-rows_all, lax.all_gather(column_recv, "section", axis=0, tiled=True))

    half = narrow_count * row_tiles

    def block_of(other):
        def make():
            own = (lax.axis_index("narrow") & 1) ^ other
            return lambda q: q + (q // half + own) * half

        return make

    away, table, scaled = sweep(blocks // 2, block_of(1))
    kept = pick_call(index, table, scaled, pairs, blocks // 2, block_of(0))
    flip = lambda bit: [(i, i ^ bit) for i in range(4)]
    summed = kept + lax.ppermute(away, "narrow", flip(1))
    opposite = lax.ppermute(summed, "narrow", flip(2))
    own, to_wide, to_narrow, to_both = arrange_call(summed, opposite, row_tiles)
    from_wide = lax.ppermute(to_wide, "wide", [(0, 1), (1, 0)])
    from_narrow = lax.ppermute(to_narrow, "narrow", flip(1))
    from_both = lax.ppermute(to_both, ("wide", "narrow"), [(i, i ^ 5) for i in range(8)])
    near = jnp.stack([own, from_wide, from_narrow, from_both])
    across = lax.ppermute(near, "section", flip(2))
    core = lax.ppermute(near, "section", flip(1))
    far = lax.ppermute(across, "section", flip(1))
    return product_call((near, across, core, far), row_tiles)


def solution(mesh):
    in_specs = (
        P(None, "narrow", None),
        P(("section", "wide"), "narrow", None),
        P(),
        P(),
        P(),
        P(("section", "wide"), None),
        P(),
    )
    out_specs = P(("section", "narrow"), "wide")
    return jax.shard_map(on_device, mesh=mesh, in_specs=in_specs, out_specs=out_specs, check_vma=False)
```

```python
import functools
import math

import jax
import jax.numpy as jnp
import numpy as np
from jax import lax
from jax.experimental import pallas as pl
from jax.experimental.pallas import tpu as pltpu
from jax.sharding import PartitionSpec as P

LANES = 128
ROWS = 8
F32 = jnp.float32
BF16 = jnp.bfloat16


def cosine_table(length):
    wavenumber = np.arange(length, dtype=np.float64)[:, None]
    position = np.arange(length, dtype=np.float64)[None, :]
    table = math.sqrt(2.0 / length) * np.cos(
        math.pi * (2.0 * position + 1.0) * wavenumber / (2.0 * length)
    )
    table[0] *= math.sqrt(0.5)
    return table.astype(np.float32)


def split(value):
    high = value.astype(BF16)
    low = (value - high.astype(F32)).astype(BF16)
    return high, low


def z_weights(cosine, per_chunk, slot):
    extent = cosine.shape[0]
    out = np.zeros((per_chunk * extent, per_chunk * slot), np.float32)
    for y in range(per_chunk):
        out[y * extent : (y + 1) * extent, y * slot : y * slot + extent] = cosine.T
    return out


def y_weights(cosine):
    extent = cosine.shape[0]
    half = cosine[:, : extent // 2].reshape(extent * extent // 4, 2)
    return np.repeat(half, LANES // 2, axis=1)


def x_tables(cosine, planes, pairs):
    extent = cosine.shape[0]
    out = np.zeros((extent // planes, planes * pairs, LANES), np.float32)
    for part in range(extent // planes):
        block = cosine[:, part * planes : (part + 1) * planes].T
        out[part, :, :extent] = np.repeat(block, pairs, axis=0)
    return out


def pick_blocks(pairs, count, block_of, table_ref, out_ref, basis_ref, lane_ref, chunk_ref, first_ref):
    rows = table_ref.shape[1]
    per_plane = basis_ref.shape[0] // rows
    tiles = rows // ROWS
    scaled_ref = table_ref.at[per_plane]
    for s in range(per_plane):
        high, low = split(table_ref[s])
        basis_ref[pl.ds(s * rows, rows), pl.ds(0, LANES)] = high
        basis_ref[pl.ds(s * rows, rows), pl.ds(LANES, LANES)] = low
    index = table_ref[per_plane + 1 :].reshape(-1, LANES)[: lane_ref.shape[0]].astype(jnp.int32)
    lane_ref[...] = index & (LANES - 1)
    upper = index >> (LANES.bit_length() - 1)
    plane = (upper * ((1 << 16) // per_plane + 1)) >> 16
    first_ref[...] = plane
    chunk_ref[...] = upper - plane * per_plane
    take = functools.partial(jnp.take_along_axis, axis=1, mode="promise_in_bounds")
    wide = 2 * LANES
    inside = lax.broadcasted_iota(jnp.int32, (LANES, wide), 0).astype(F32).astype(BF16)
    one = jnp.ones((), BF16)
    zero = jnp.zeros((), BF16)

    def row_of(ref, b):
        return jnp.broadcast_to(ref[pl.ds(b, 1), :], (ROWS, LANES))

    def select(chunk, candidate):
        picked = [None] * tiles
        for c in range(per_plane):
            mine = chunk == c
            for t in range(tiles):
                found = candidate(c, t)
                picked[t] = found if c == 0 else jnp.where(mine, found, picked[t])
        return picked

    def finish(q, b, picked):
        first = row_of(first_ref, b)
        out = None
        for t in range(tiles):
            term = picked[t] * take(scaled_ref[pl.ds(t * ROWS, ROWS), :], first)
            out = term if out is None else out + term
        out = out + pltpu.roll(out, pairs, 0)
        out_ref[q] = out[:pairs]

    def three(step, carry):
        places = [step * 3 + u for u in range(3)]
        ids = [block_of(q) for q in places]
        lane = jnp.concatenate([lane_ref[pl.ds(b, 1), :] for b in ids[:2]], axis=1)
        hot = jnp.where(inside == lane.astype(F32).astype(BF16), one, zero)
        offers = jnp.dot(basis_ref[...], jnp.concatenate([hot, hot], axis=0), preferred_element_type=F32)
        third_lane = row_of(lane_ref, ids[2])
        third = select(row_of(chunk_ref, ids[2]), lambda c, t: take(table_ref[c, pl.ds(t * ROWS, ROWS), :], third_lane))
        chunk = jnp.concatenate([row_of(chunk_ref, b) for b in ids[:2]], axis=1)
        picked = select(chunk, lambda c, t: offers[c * rows + t * ROWS : c * rows + (t + 1) * ROWS])
        for u in range(2):
            finish(places[u], ids[u], [value[:, u * LANES : (u + 1) * LANES] for value in picked])
        finish(places[2], ids[2], third)
        return carry

    lax.fori_loop(0, count // 3, three, 0, unroll=8)


def sweep_kernel(
    sizes,
    *refs,
):
    given, (out_ref, kept_ref), held = refs[:11], refs[11:13], refs[13:24]
    table_ref, density_ref, fold_ref, *picking, sems, store_sem = refs[24:]
    store = pltpu.make_async_copy(table_ref, kept_ref, store_sem)
    loads = [pltpu.make_async_copy(source, target, sems.at[i]) for i, (source, target) in enumerate(zip(given, held))]
    for load in loads:
        load.start()
    bands_ref, valence_energy_ref, conduction_energy_ref, frequency_ref, *held = held
    valence_ref, conduction_ref, z_high_ref, z_low_ref, y_ref, x_ref, index_ref = held
    for load in loads[:4]:
        load.wait()
    loads = loads[4:]
    extent, planes, pairs, total_pairs, count, block_of = sizes
    rows = planes * pairs
    tiles = rows // ROWS
    per_tile = ROWS // pairs
    per_chunk = 3 * LANES // extent
    groups = extent // per_chunk
    row_id = lax.broadcasted_iota(jnp.int32, (ROWS, LANES), 0)
    lane_id = lax.broadcasted_iota(jnp.int32, (ROWS, LANES), 1)
    band = jnp.zeros((ROWS, LANES), jnp.int32)
    for p in range(pairs):
        band = jnp.where(row_id % pairs == p, bands_ref[0, p], band)
    loads[0].wait()
    loads[1].wait()
    for m in range(groups):
        for part in range(3):
            lanes = pl.ds((m * 3 + part) * LANES, LANES)
            for t in range(tiles):
                value, factor = None, None
                for u in range(per_tile):
                    plane = t * per_tile + u
                    picked = jnp.take_along_axis(valence_ref[plane, :, lanes], band, axis=0, mode="promise_in_bounds")
                    other = jnp.broadcast_to(conduction_ref[plane, :, lanes], (ROWS, LANES))
                    value = picked if u == 0 else jnp.where(row_id >= u * pairs, picked, value)
                    factor = other if u == 0 else jnp.where(row_id >= u * pairs, other, factor)
                density_ref[part, pl.ds(m * rows + t * ROWS, ROWS), :] = value * factor
    density = jnp.concatenate([density_ref[part] for part in range(3)], axis=1)
    high, low = split(density)
    loads[2].wait()
    loads[3].wait()
    dot = functools.partial(jnp.dot, preferred_element_type=F32)
    swept = dot(high, z_high_ref[...]) + dot(low, z_high_ref[...]) + dot(high, z_low_ref[...])
    quarter = per_chunk // 2
    for m in range(groups // 2):
        for q in range(quarter):
            near = swept[m * rows : (m + 1) * rows, q * LANES : (q + 1) * LANES]
            far_m, far_q = groups - 1 - m, quarter - 1 - q
            far = swept[far_m * rows : (far_m + 1) * rows, far_q * LANES : (far_q + 1) * LANES]
            far = pltpu.roll(far, LANES // 2, 1)
            fold_ref[0, m * quarter + q] = near + far
            fold_ref[1, m * quarter + q] = near - far
    terms = extent // 4
    block = 2 * ROWS
    loads[4].wait()

    def sweep_tiles(t, carry):
        where_rows = pl.ds(pl.multiple_of(t * block, block), block)
        for parity in range(2):
            parts = [fold_ref[parity, s, where_rows, :] for s in range(terms)]
            for j in range(parity, extent, 2):
                total = None
                for s in range(terms):
                    term = parts[s] * y_ref[pl.ds(j * terms + s, 1), :]
                    total = term if total is None else total + term
                total = total + pltpu.roll(total, LANES // 2, 1)
                start = j * extent
                offset = start % LANES
                moved = total if offset % (LANES // 2) == 0 else pltpu.roll(total, offset, 1)
                for chunk in range(start // LANES, (start + extent - 1) // LANES + 1):
                    low_lane = max(start - chunk * LANES, 0)
                    high_lane = min(start + extent - chunk * LANES, LANES)
                    table_ref[chunk, where_rows, low_lane:high_lane] = moved[:, low_lane:high_lane]
        return carry

    lax.fori_loop(0, rows // block, sweep_tiles, 0)
    per_plane = extent * extent // LANES
    loads[5].wait()
    loads[6].wait()
    narrow_pos = lax.axis_index("narrow")
    gap = jnp.zeros((ROWS, LANES), F32)
    for p in range(pairs):
        one_gap = conduction_energy_ref[bands_ref[1, p]] - valence_energy_ref[bands_ref[0, p]]
        gap = jnp.where(row_id % pairs == p, one_gap, gap)
    frequency = frequency_ref[0]
    scale = jnp.sqrt(4.0 * gap / (gap * gap + frequency * frequency) / math.sqrt(total_pairs))
    for t in range(tiles):
        table_ref[per_plane, pl.ds(t * ROWS, ROWS), :] = x_ref[narrow_pos, pl.ds(t * ROWS, ROWS), :] * scale
    blocks = index_ref.shape[0]
    for i in range(table_ref.shape[0] - per_plane - 1):
        some = min(rows, blocks - i * rows)
        table_ref[per_plane + 1 + i, pl.ds(0, some), :] = index_ref[pl.ds(i * rows, some), :].astype(F32)
    store.start()
    pick_blocks(pairs, count, block_of(), table_ref, out_ref, *picking)
    store.wait()


def pick_kernel(pairs, count, block_of, *refs):
    pick_blocks(pairs, count, block_of(), *refs)


def pick_scratch(blocks, rows, area):
    return [pltpu.VMEM((area // LANES * rows, 2 * LANES), BF16)] + [pltpu.VMEM((blocks, LANES), jnp.int32)] * 3


VMEM = pl.BlockSpec(memory_space=pltpu.VMEM)
HBM = pl.BlockSpec(memory_space=pltpu.HBM)


def sweep_call(bands, valence_energy, conduction_energy, frequency, valence, conduction, index, total_pairs, count, block_of):
    pairs = bands.shape[1]
    planes, area = valence.shape[0], valence.shape[2]
    extent = math.isqrt(area)
    rows = planes * pairs
    cosine = cosine_table(extent)
    per_chunk = 3 * LANES // extent
    groups = extent // per_chunk
    weights = z_weights(cosine, per_chunk, LANES // 2)
    z_high = weights.astype(BF16)
    z_low = (weights - z_high.astype(np.float32)).astype(BF16)
    operands = [valence, conduction, jnp.asarray(z_high), jnp.asarray(z_low)]
    operands += [jnp.asarray(y_weights(cosine)), jnp.asarray(x_tables(cosine, planes, pairs)), index]
    chunks = area // LANES
    blocks = index.shape[0]
    table = jax.ShapeDtypeStruct((area // LANES + 1 + -(-blocks // rows), rows, LANES), F32)
    scalars = [bands, valence_energy, conduction_energy, frequency]
    return pl.pallas_call(
        functools.partial(sweep_kernel, (extent, planes, pairs, total_pairs, count, block_of)),
        out_shape=[jax.ShapeDtypeStruct((count, pairs, LANES), F32), table],
        in_specs=[HBM] * (len(scalars) + len(operands)),
        out_specs=[VMEM, HBM],
        scratch_shapes=[pltpu.SMEM(a.shape, a.dtype) for a in scalars]
        + [pltpu.VMEM(a.shape, a.dtype) for a in operands]
        + [
            pltpu.VMEM(table.shape, F32),
            pltpu.VMEM((3, groups * rows, LANES), F32),
            pltpu.VMEM((2, extent // 4, rows, LANES), F32),
        ]
        + pick_scratch(blocks, rows, area)
        + [pltpu.SemaphoreType.DMA((len(scalars) + len(operands),)), pltpu.SemaphoreType.DMA],
        cost_estimate=pl.CostEstimate(flops=8_000_000_000, bytes_accessed=4_000_000, transcendentals=0),
        name="sweep",
    )(*scalars, *operands)


def pick_call(table, blocks, area, pairs, count, block_of):
    return pl.pallas_call(
        functools.partial(pick_kernel, pairs, count, block_of),
        out_shape=jax.ShapeDtypeStruct((count, pairs, LANES), F32),
        in_specs=[VMEM],
        out_specs=VMEM,
        scratch_shapes=pick_scratch(blocks, table.shape[1], area),
        compiler_params=pltpu.CompilerParams(vmem_limit_bytes=32 << 20),
        cost_estimate=pl.CostEstimate(flops=4_000_000_000, bytes_accessed=1_000_000, transcendentals=0),
        name="pick",
    )(table)


def arrange_kernel(row_tiles, near_ref, far_ref, own_ref, wide_ref, narrow_ref, both_ref):
    narrow_count = lax.axis_size("narrow")
    half = narrow_count * row_tiles
    wide_pos, narrow_pos = lax.axis_index("wide"), lax.axis_index("narrow")
    for out_ref, w, n in (
        (own_ref, wide_pos, narrow_pos),
        (wide_ref, 1 - wide_pos, narrow_pos),
        (narrow_ref, wide_pos, narrow_pos ^ 1),
        (both_ref, 1 - wide_pos, narrow_pos ^ 1),
    ):
        columns = pl.ds(w * half, half)
        rows = pl.ds((1 - w) * half + n * row_tiles, row_tiles)
        out_ref[pl.ds(0, half)] = near_ref[columns] + far_ref[columns]
        out_ref[pl.ds(half, row_tiles)] = near_ref[rows] + far_ref[rows]


def arrange_call(near, far, row_tiles):
    blocks, pairs, _ = near.shape
    shape = (blocks // 2 + row_tiles, pairs, LANES)
    return pl.pallas_call(
        functools.partial(arrange_kernel, row_tiles),
        out_shape=[jax.ShapeDtypeStruct(shape, F32)] * 4,
        in_specs=[VMEM] * 2,
        out_specs=[VMEM] * 4,
        compiler_params=pltpu.CompilerParams(vmem_limit_bytes=16 << 20),
        name="arrange",
    )(near, far)


def product_kernel(row_tiles, pairs, own_ref, across_ref, core_ref, far_ref, out_ref, rows_ref, gather_ref, value_ref, sems):
    section, wide_pos, narrow_pos = lax.axis_index("section"), lax.axis_index("wide"), lax.axis_index("narrow")
    parity = narrow_pos & 1
    narrow_count = lax.axis_size("narrow")
    half = narrow_count * row_tiles
    sources = (own_ref, across_ref, core_ref, far_ref)
    row_block = rows_ref.shape[0]

    def collect(kind, start):
        for i, ref in enumerate(sources):
            for b in range(2):
                rows = pl.ds((2 * i + b) * pairs, pairs)
                for r in range(row_tiles):
                    gather_ref[rows, pl.ds(r * LANES, LANES)] = ref[2 * kind + b, start + r]
        return gather_ref[...]

    start = jnp.where(section // 2 == wide_pos, narrow_pos * row_tiles, half)
    high, low = split(-collect((section & 1) ^ parity, start))
    high, low = high.astype(F32), low.astype(F32)
    rows_ref[...] = jnp.concatenate([high, high, low, low], axis=0).T.astype(BF16)

    def copy_of(step):
        columns = pl.ds(pl.multiple_of(step * row_block, row_block), row_block)
        return pltpu.make_async_copy(value_ref.at[:, columns], out_ref.at[:, columns], sems.at[step])

    def one_block(step, carry):
        high, low = split(collect((step // narrow_count) ^ parity, (step % narrow_count) * row_tiles))
        stacked = jnp.concatenate([high, low, high, low], axis=0)
        columns = pl.ds(pl.multiple_of(step * row_block, row_block), row_block)
        value_ref[:, columns] = jnp.dot(rows_ref[...], stacked, preferred_element_type=F32)
        copy_of(step).start()
        return carry

    def wait_block(step, carry):
        copy_of(step).wait()
        return carry

    steps = 2 * narrow_count
    lax.fori_loop(0, steps, one_block, 0)
    lax.fori_loop(0, steps, wait_block, 0)


def product_call(sources, row_tiles):
    _, blocks, pairs, _ = sources[0].shape
    row_block = row_tiles * LANES
    steps = 2 * (blocks // row_tiles - 1)
    depth = 2 * len(sources) * pairs
    return pl.pallas_call(
        functools.partial(product_kernel, row_tiles, pairs),
        out_shape=jax.ShapeDtypeStruct((row_block, steps * row_block), F32),
        in_specs=[VMEM] * len(sources),
        out_specs=pl.BlockSpec(memory_space=pl.ANY),
        scratch_shapes=[
            pltpu.VMEM((row_block, 4 * depth), BF16),
            pltpu.VMEM((depth, row_block), F32),
            pltpu.VMEM((row_block, steps * row_block), F32),
            pltpu.SemaphoreType.DMA((steps,)),
        ],
        compiler_params=pltpu.CompilerParams(vmem_limit_bytes=40 << 20),
        name="product",
    )(*sources)


def contract(left_rows, right_rows):
    return lax.dot_general(
        left_rows,
        right_rows,
        (((0,), (0,)), ((), ())),
        precision=lax.Precision.HIGHEST,
        preferred_element_type=F32,
    )


def on_device(valence, conduction, valence_energy, conduction_energy, frequency, pair_bands, gvec_index):
    pairs = pair_bands.shape[0]
    section_count, wide_count, narrow_count = (lax.axis_size(name) for name in ("section", "wide", "narrow"))
    total_pairs = pairs * section_count * wide_count
    vector_count = gvec_index.shape[0]
    row_block = vector_count // (section_count * narrow_count)
    column_block = vector_count // wide_count
    row_tiles = row_block // LANES
    blocks = vector_count // LANES
    index = gvec_index.reshape(blocks, LANES)
    valence, conduction = (jnp.swapaxes(orbitals, 0, 1) for orbitals in (valence, conduction))
    energies = (valence_energy, conduction_energy, frequency)
    sweep = functools.partial(sweep_call, pair_bands.T, *energies, valence, conduction, index, total_pairs)

    if not (section_count == 4 and wide_count == 2 and narrow_count == 4):
        partial_value = sweep(blocks, lambda: lambda q: q)[0]
        partial_value = jnp.swapaxes(partial_value, 0, 1).reshape(pairs, section_count, narrow_count, row_block)
        own_rows = lax.psum_scatter(partial_value, "narrow", scatter_dimension=2, tiled=True)
        coefficients = lax.all_gather(own_rows, "narrow", axis=2, tiled=True).reshape(pairs, vector_count)
        row_send = own_rows.reshape(pairs, section_count, row_block)
        row_recv = lax.all_to_all(row_send, "section", split_axis=1, concat_axis=0, tiled=True)
        row_recv = row_recv.reshape(section_count, pairs, row_block)
        column_send = coefficients.reshape(pairs, wide_count, column_block)
        column_recv = lax.all_to_all(column_send, "wide", split_axis=1, concat_axis=0, tiled=True)
        column_recv = column_recv.reshape(wide_count * pairs, column_block)
        rows_all = lax.all_gather(row_recv, "wide", axis=1, tiled=True).reshape(-1, row_block)
        return contract(-rows_all, lax.all_gather(column_recv, "section", axis=0, tiled=True))

    half = narrow_count * row_tiles

    def block_of(other):
        def make():
            own = (lax.axis_index("narrow") & 1) ^ other
            return lambda q: q + (q // half + own) * half

        return make

    away, table = sweep(blocks // 2, block_of(1))
    kept = pick_call(table, blocks, valence.shape[2], pairs, blocks // 2, block_of(0))
    flip = lambda bit: [(i, i ^ bit) for i in range(4)]
    summed = kept + lax.ppermute(away, "narrow", flip(1))
    opposite = lax.ppermute(summed, "narrow", flip(2))
    own, to_wide, to_narrow, to_both = arrange_call(summed, opposite, row_tiles)
    from_wide = lax.ppermute(to_wide, "wide", [(0, 1), (1, 0)])
    from_narrow = lax.ppermute(to_narrow, "narrow", flip(1))
    from_both = lax.ppermute(to_both, ("wide", "narrow"), [(i, i ^ 5) for i in range(8)])
    near = jnp.stack([own, from_wide, from_narrow, from_both])
    across = lax.ppermute(near, "section", flip(2))
    core = lax.ppermute(near, "section", flip(1))
    far = lax.ppermute(across, "section", flip(1))
    return product_call((near, across, core, far), row_tiles)


def solution(mesh):
    in_specs = (
        P(None, "narrow", None),
        P(("section", "wide"), "narrow", None),
        P(),
        P(),
        P(),
        P(("section", "wide"), None),
        P(),
    )
    out_specs = P(("section", "narrow"), "wide")
    return jax.shard_map(on_device, mesh=mesh, in_specs=in_specs, out_specs=out_specs, check_vma=False)
```

```python
import functools
import math

import jax
import jax.numpy as jnp
import numpy as np
from jax import lax
from jax.experimental import pallas as pl
from jax.experimental.pallas import tpu as pltpu
from jax.sharding import PartitionSpec as P

LANES = 128
ROWS = 8
F32 = jnp.float32
BF16 = jnp.bfloat16


def cosine_table(length):
    wavenumber = np.arange(length, dtype=np.float64)[:, None]
    position = np.arange(length, dtype=np.float64)[None, :]
    table = math.sqrt(2.0 / length) * np.cos(
        math.pi * (2.0 * position + 1.0) * wavenumber / (2.0 * length)
    )
    table[0] *= math.sqrt(0.5)
    return table.astype(np.float32)


def split(value):
    high = value.astype(BF16)
    low = (value - high.astype(F32)).astype(BF16)
    return high, low


def z_weights(cosine, per_chunk, slot):
    extent = cosine.shape[0]
    out = np.zeros((per_chunk * extent, per_chunk * slot), np.float32)
    for y in range(per_chunk):
        out[y * extent : (y + 1) * extent, y * slot : y * slot + extent] = cosine.T
    return out


def y_weights(cosine):
    extent = cosine.shape[0]
    half = cosine[:, : extent // 2].reshape(extent * extent // 4, 2)
    return np.repeat(half, LANES // 2, axis=1)


def x_tables(cosine, planes, pairs):
    extent = cosine.shape[0]
    out = np.zeros((extent // planes, planes * pairs, LANES), np.float32)
    for part in range(extent // planes):
        block = cosine[:, part * planes : (part + 1) * planes].T
        out[part, :, :extent] = np.repeat(block, pairs, axis=0)
    return out


def pick_blocks(pairs, count, block_of, table_ref, out_ref, basis_ref, lane_ref, chunk_ref, first_ref):
    rows = table_ref.shape[1]
    per_plane = basis_ref.shape[0] // rows
    tiles = rows // ROWS
    scaled_ref = table_ref.at[per_plane]
    for s in range(per_plane):
        high, low = split(table_ref[s])
        basis_ref[pl.ds(s * rows, rows), pl.ds(0, LANES)] = high
        basis_ref[pl.ds(s * rows, rows), pl.ds(LANES, LANES)] = low
    index = table_ref[per_plane + 1 :].reshape(-1, LANES)[: lane_ref.shape[0]].astype(jnp.int32)
    lane_ref[...] = index & (LANES - 1)
    upper = index >> (LANES.bit_length() - 1)
    plane = (upper * ((1 << 16) // per_plane + 1)) >> 16
    first_ref[...] = plane
    chunk_ref[...] = upper - plane * per_plane
    take = functools.partial(jnp.take_along_axis, axis=1, mode="promise_in_bounds")
    wide = 2 * LANES
    inside = lax.broadcasted_iota(jnp.int32, (LANES, wide), 0).astype(F32).astype(BF16)
    one = jnp.ones((), BF16)
    zero = jnp.zeros((), BF16)

    def row_of(ref, b):
        return jnp.broadcast_to(ref[pl.ds(b, 1), :], (ROWS, LANES))

    def select(chunk, candidate):
        picked = [None] * tiles
        for c in range(per_plane):
            mine = chunk == c
            for t in range(tiles):
                found = candidate(c, t)
                picked[t] = found if c == 0 else jnp.where(mine, found, picked[t])
        return picked

    def finish(q, b, picked):
        first = row_of(first_ref, b)
        out = None
        for t in range(tiles):
            term = picked[t] * take(scaled_ref[pl.ds(t * ROWS, ROWS), :], first)
            out = term if out is None else out + term
        out = out + pltpu.roll(out, pairs, 0)
        out_ref[q] = out[:pairs]

    def three(step, carry):
        places = [step * 3 + u for u in range(3)]
        ids = [block_of(q) for q in places]
        lane = jnp.concatenate([lane_ref[pl.ds(b, 1), :] for b in ids[:2]], axis=1)
        hot = jnp.where(inside == lane.astype(F32).astype(BF16), one, zero)
        offers = jnp.dot(basis_ref[...], jnp.concatenate([hot, hot], axis=0), preferred_element_type=F32)
        third_lane = row_of(lane_ref, ids[2])
        third = select(row_of(chunk_ref, ids[2]), lambda c, t: take(table_ref[c, pl.ds(t * ROWS, ROWS), :], third_lane))
        chunk = jnp.concatenate([row_of(chunk_ref, b) for b in ids[:2]], axis=1)
        picked = select(chunk, lambda c, t: offers[c * rows + t * ROWS : c * rows + (t + 1) * ROWS])
        for u in range(2):
            finish(places[u], ids[u], [value[:, u * LANES : (u + 1) * LANES] for value in picked])
        finish(places[2], ids[2], third)
        return carry

    lax.fori_loop(0, count // 3, three, 0, unroll=16)


def sweep_kernel(
    sizes,
    *refs,
):
    given, (out_ref, table_ref), held = refs[:11], refs[11:13], refs[13:24]
    density_ref, fold_ref, *picking, sems = refs[24:]
    loads = [pltpu.make_async_copy(source, target, sems.at[i]) for i, (source, target) in enumerate(zip(given, held))]
    for load in loads[4:6] + loads[:4] + loads[6:]:
        load.start()
    bands_ref, valence_energy_ref, conduction_energy_ref, frequency_ref, *held = held
    valence_ref, conduction_ref, z_high_ref, z_low_ref, y_ref, x_ref, index_ref = held
    for load in loads[:4]:
        load.wait()
    loads = loads[4:]
    extent, planes, pairs, total_pairs, count, block_of = sizes
    rows = planes * pairs
    tiles = rows // ROWS
    per_tile = ROWS // pairs
    per_chunk = 3 * LANES // extent
    groups = extent // per_chunk
    row_id = lax.broadcasted_iota(jnp.int32, (ROWS, LANES), 0)
    lane_id = lax.broadcasted_iota(jnp.int32, (ROWS, LANES), 1)
    band = jnp.zeros((ROWS, LANES), jnp.int32)
    for p in range(pairs):
        band = jnp.where(row_id % pairs == p, bands_ref[0, p], band)
    loads[0].wait()
    loads[1].wait()
    for m in range(groups):
        for part in range(3):
            lanes = pl.ds((m * 3 + part) * LANES, LANES)
            for t in range(tiles):
                value, factor = None, None
                for u in range(per_tile):
                    plane = t * per_tile + u
                    picked = jnp.take_along_axis(valence_ref[plane, :, lanes], band, axis=0, mode="promise_in_bounds")
                    other = jnp.broadcast_to(conduction_ref[plane, :, lanes], (ROWS, LANES))
                    value = picked if u == 0 else jnp.where(row_id >= u * pairs, picked, value)
                    factor = other if u == 0 else jnp.where(row_id >= u * pairs, other, factor)
                density_ref[part, pl.ds(m * rows + t * ROWS, ROWS), :] = value * factor
    density = jnp.concatenate([density_ref[part] for part in range(3)], axis=1)
    high, low = split(density)
    loads[2].wait()
    loads[3].wait()
    dot = functools.partial(jnp.dot, preferred_element_type=F32)
    swept = dot(high, z_high_ref[...]) + dot(low, z_high_ref[...]) + dot(high, z_low_ref[...])
    quarter = per_chunk // 2
    for m in range(groups // 2):
        for q in range(quarter):
            near = swept[m * rows : (m + 1) * rows, q * LANES : (q + 1) * LANES]
            far_m, far_q = groups - 1 - m, quarter - 1 - q
            far = swept[far_m * rows : (far_m + 1) * rows, far_q * LANES : (far_q + 1) * LANES]
            far = pltpu.roll(far, LANES // 2, 1)
            fold_ref[0, m * quarter + q] = near + far
            fold_ref[1, m * quarter + q] = near - far
    terms = extent // 4
    block = 2 * ROWS
    loads[4].wait()

    def sweep_tiles(t, carry):
        where_rows = pl.ds(pl.multiple_of(t * block, block), block)
        for parity in range(2):
            parts = [fold_ref[parity, s, where_rows, :] for s in range(terms)]
            for j in range(parity, extent, 2):
                total = None
                for s in range(terms):
                    term = parts[s] * y_ref[pl.ds(j * terms + s, 1), :]
                    total = term if total is None else total + term
                total = total + pltpu.roll(total, LANES // 2, 1)
                start = j * extent
                offset = start % LANES
                moved = total if offset % (LANES // 2) == 0 else pltpu.roll(total, offset, 1)
                for chunk in range(start // LANES, (start + extent - 1) // LANES + 1):
                    low_lane = max(start - chunk * LANES, 0)
                    high_lane = min(start + extent - chunk * LANES, LANES)
                    table_ref[chunk, where_rows, low_lane:high_lane] = moved[:, low_lane:high_lane]
        return carry

    lax.fori_loop(0, rows // block, sweep_tiles, 0)
    per_plane = extent * extent // LANES
    loads[5].wait()
    loads[6].wait()
    narrow_pos = lax.axis_index("narrow")
    gap = jnp.zeros((ROWS, LANES), F32)
    for p in range(pairs):
        one_gap = conduction_energy_ref[bands_ref[1, p]] - valence_energy_ref[bands_ref[0, p]]
        gap = jnp.where(row_id % pairs == p, one_gap, gap)
    frequency = frequency_ref[0]
    scale = jnp.sqrt(4.0 * gap / (gap * gap + frequency * frequency) / math.sqrt(total_pairs))
    for t in range(tiles):
        table_ref[per_plane, pl.ds(t * ROWS, ROWS), :] = x_ref[narrow_pos, pl.ds(t * ROWS, ROWS), :] * scale
    blocks = index_ref.shape[0]
    for i in range(table_ref.shape[0] - per_plane - 1):
        some = min(rows, blocks - i * rows)
        table_ref[per_plane + 1 + i, pl.ds(0, some), :] = index_ref[pl.ds(i * rows, some), :].astype(F32)
    pick_blocks(pairs, count, block_of(), table_ref, out_ref, *picking)


def pick_kernel(pairs, count, block_of, *refs):
    pick_blocks(pairs, count, block_of(), *refs)


def pick_scratch(blocks, rows, area):
    return [pltpu.VMEM((area // LANES * rows, 2 * LANES), BF16)] + [pltpu.VMEM((blocks, LANES), jnp.int32)] * 3


VMEM = pl.BlockSpec(memory_space=pltpu.VMEM)
HBM = pl.BlockSpec(memory_space=pltpu.HBM)
ANY = pl.BlockSpec(memory_space=pl.ANY)


def sweep_call(bands, valence_energy, conduction_energy, frequency, valence, conduction, index, total_pairs, count, block_of):
    pairs = bands.shape[1]
    planes, area = valence.shape[0], valence.shape[2]
    extent = math.isqrt(area)
    rows = planes * pairs
    cosine = cosine_table(extent)
    per_chunk = 3 * LANES // extent
    groups = extent // per_chunk
    weights = z_weights(cosine, per_chunk, LANES // 2)
    z_high = weights.astype(BF16)
    z_low = (weights - z_high.astype(np.float32)).astype(BF16)
    operands = [valence, conduction, jnp.asarray(z_high), jnp.asarray(z_low)]
    operands += [jnp.asarray(y_weights(cosine)), jnp.asarray(x_tables(cosine, planes, pairs)), index]
    chunks = area // LANES
    blocks = index.shape[0]
    table = jax.ShapeDtypeStruct((area // LANES + 1 + -(-blocks // rows), rows, LANES), F32)
    scalars = [bands, valence_energy, conduction_energy, frequency]
    return pl.pallas_call(
        functools.partial(sweep_kernel, (extent, planes, pairs, total_pairs, count, block_of)),
        out_shape=[jax.ShapeDtypeStruct((count, pairs, LANES), F32), table],
        in_specs=[HBM] * 3 + [ANY] + [HBM] * len(operands),
        out_specs=[VMEM, VMEM],
        scratch_shapes=[pltpu.SMEM(a.shape, a.dtype) for a in scalars]
        + [pltpu.VMEM(a.shape, a.dtype) for a in operands]
        + [
            pltpu.VMEM((3, groups * rows, LANES), F32),
            pltpu.VMEM((2, extent // 4, rows, LANES), F32),
        ]
        + pick_scratch(blocks, rows, area)
        + [pltpu.SemaphoreType.DMA((len(scalars) + len(operands),))],
        compiler_params=pltpu.CompilerParams(vmem_limit_bytes=32 << 20),
        cost_estimate=pl.CostEstimate(flops=8_000_000_000, bytes_accessed=4_000_000, transcendentals=0),
        name="sweep",
    )(*(a if a is frequency else pltpu.with_memory_space_constraint(a, pltpu.HBM) for a in (*scalars, *operands)))


def pick_call(table, blocks, area, pairs, count, block_of):
    return pl.pallas_call(
        functools.partial(pick_kernel, pairs, count, block_of),
        out_shape=jax.ShapeDtypeStruct((count, pairs, LANES), F32),
        in_specs=[VMEM],
        out_specs=VMEM,
        scratch_shapes=pick_scratch(blocks, table.shape[1], area),
        compiler_params=pltpu.CompilerParams(vmem_limit_bytes=32 << 20),
        cost_estimate=pl.CostEstimate(flops=4_000_000_000, bytes_accessed=1_000_000, transcendentals=0),
        name="pick",
    )(table)


def arrange_kernel(row_tiles, near_ref, far_ref, own_ref, wide_ref, narrow_ref, both_ref):
    narrow_count = lax.axis_size("narrow")
    half = narrow_count * row_tiles
    wide_pos, narrow_pos = lax.axis_index("wide"), lax.axis_index("narrow")
    for out_ref, w, n in (
        (own_ref, wide_pos, narrow_pos),
        (wide_ref, 1 - wide_pos, narrow_pos),
        (narrow_ref, wide_pos, narrow_pos ^ 1),
        (both_ref, 1 - wide_pos, narrow_pos ^ 1),
    ):
        columns = pl.ds(w * half, half)
        rows = pl.ds((1 - w) * half + n * row_tiles, row_tiles)
        out_ref[pl.ds(0, half)] = near_ref[columns] + far_ref[columns]
        out_ref[pl.ds(half, row_tiles)] = near_ref[rows] + far_ref[rows]


def arrange_call(near, far, row_tiles):
    blocks, pairs, _ = near.shape
    shape = (blocks // 2 + row_tiles, pairs, LANES)
    return pl.pallas_call(
        functools.partial(arrange_kernel, row_tiles),
        out_shape=[jax.ShapeDtypeStruct(shape, F32)] * 4,
        in_specs=[VMEM] * 2,
        out_specs=[VMEM] * 4,
        compiler_params=pltpu.CompilerParams(vmem_limit_bytes=16 << 20),
        name="arrange",
    )(near, far)


def product_kernel(row_tiles, pairs, own_ref, across_ref, core_ref, far_ref, out_ref, rows_ref, gather_ref, value_ref, sems):
    section, wide_pos, narrow_pos = lax.axis_index("section"), lax.axis_index("wide"), lax.axis_index("narrow")
    parity = narrow_pos & 1
    narrow_count = lax.axis_size("narrow")
    half = narrow_count * row_tiles
    sources = (own_ref, across_ref, core_ref, far_ref)
    row_block = rows_ref.shape[0]

    def collect(kind, start):
        for i, ref in enumerate(sources):
            for b in range(2):
                rows = pl.ds((2 * i + b) * pairs, pairs)
                for r in range(row_tiles):
                    gather_ref[rows, pl.ds(r * LANES, LANES)] = ref[2 * kind + b, start + r]
        return gather_ref[...]

    start = jnp.where(section // 2 == wide_pos, narrow_pos * row_tiles, half)
    high, low = split(-collect((section & 1) ^ parity, start))
    high, low = high.astype(F32), low.astype(F32)
    rows_ref[...] = jnp.concatenate([high, high, low, low], axis=0).T.astype(BF16)

    def copy_of(step):
        columns = pl.ds(pl.multiple_of(step * row_block, row_block), row_block)
        return pltpu.make_async_copy(value_ref.at[:, columns], out_ref.at[:, columns], sems.at[step])

    def one_block(step, carry):
        high, low = split(collect((step // narrow_count) ^ parity, (step % narrow_count) * row_tiles))
        stacked = jnp.concatenate([high, low, high, low], axis=0)
        columns = pl.ds(pl.multiple_of(step * row_block, row_block), row_block)
        value_ref[:, columns] = jnp.dot(rows_ref[...], stacked, preferred_element_type=F32)
        copy_of(step).start()
        return carry

    def wait_block(step, carry):
        copy_of(step).wait()
        return carry

    steps = 2 * narrow_count
    lax.fori_loop(0, steps, one_block, 0)
    lax.fori_loop(0, steps, wait_block, 0)


def product_call(sources, row_tiles):
    _, blocks, pairs, _ = sources[0].shape
    row_block = row_tiles * LANES
    steps = 2 * (blocks // row_tiles - 1)
    depth = 2 * len(sources) * pairs
    return pl.pallas_call(
        functools.partial(product_kernel, row_tiles, pairs),
        out_shape=jax.ShapeDtypeStruct((row_block, steps * row_block), F32),
        in_specs=[VMEM] * len(sources),
        out_specs=pl.BlockSpec(memory_space=pl.ANY),
        scratch_shapes=[
            pltpu.VMEM((row_block, 4 * depth), BF16),
            pltpu.VMEM((depth, row_block), F32),
            pltpu.VMEM((row_block, steps * row_block), F32),
            pltpu.SemaphoreType.DMA((steps,)),
        ],
        compiler_params=pltpu.CompilerParams(vmem_limit_bytes=40 << 20),
        name="product",
    )(*sources)


def contract(left_rows, right_rows):
    return lax.dot_general(
        left_rows,
        right_rows,
        (((0,), (0,)), ((), ())),
        precision=lax.Precision.HIGHEST,
        preferred_element_type=F32,
    )


def on_device(valence, conduction, valence_energy, conduction_energy, frequency, pair_bands, gvec_index):
    pairs = pair_bands.shape[0]
    section_count, wide_count, narrow_count = (lax.axis_size(name) for name in ("section", "wide", "narrow"))
    total_pairs = pairs * section_count * wide_count
    vector_count = gvec_index.shape[0]
    row_block = vector_count // (section_count * narrow_count)
    column_block = vector_count // wide_count
    row_tiles = row_block // LANES
    blocks = vector_count // LANES
    index = gvec_index.reshape(blocks, LANES)
    valence, conduction = (jnp.swapaxes(orbitals, 0, 1) for orbitals in (valence, conduction))
    energies = (valence_energy, conduction_energy, frequency)
    sweep = functools.partial(sweep_call, pair_bands.T, *energies, valence, conduction, index, total_pairs)

    if not (section_count == 4 and wide_count == 2 and narrow_count == 4):
        partial_value = sweep(blocks, lambda: lambda q: q)[0]
        partial_value = jnp.swapaxes(partial_value, 0, 1).reshape(pairs, section_count, narrow_count, row_block)
        own_rows = lax.psum_scatter(partial_value, "narrow", scatter_dimension=2, tiled=True)
        coefficients = lax.all_gather(own_rows, "narrow", axis=2, tiled=True).reshape(pairs, vector_count)
        row_send = own_rows.reshape(pairs, section_count, row_block)
        row_recv = lax.all_to_all(row_send, "section", split_axis=1, concat_axis=0, tiled=True)
        row_recv = row_recv.reshape(section_count, pairs, row_block)
        column_send = coefficients.reshape(pairs, wide_count, column_block)
        column_recv = lax.all_to_all(column_send, "wide", split_axis=1, concat_axis=0, tiled=True)
        column_recv = column_recv.reshape(wide_count * pairs, column_block)
        rows_all = lax.all_gather(row_recv, "wide", axis=1, tiled=True).reshape(-1, row_block)
        return contract(-rows_all, lax.all_gather(column_recv, "section", axis=0, tiled=True))

    half = narrow_count * row_tiles

    def block_of(other):
        def make():
            own = (lax.axis_index("narrow") & 1) ^ other
            return lambda q: q + (q // half + own) * half

        return make

    away, table = sweep(blocks // 2, block_of(1))
    kept = pick_call(table, blocks, valence.shape[2], pairs, blocks // 2, block_of(0))
    flip = lambda bit: [(i, i ^ bit) for i in range(4)]
    summed = kept + lax.ppermute(away, "narrow", flip(1))
    opposite = lax.ppermute(summed, "narrow", flip(2))
    own, to_wide, to_narrow, to_both = arrange_call(summed, opposite, row_tiles)
    from_wide = lax.ppermute(to_wide, "wide", [(0, 1), (1, 0)])
    from_narrow = lax.ppermute(to_narrow, "narrow", flip(1))
    from_both = lax.ppermute(to_both, ("wide", "narrow"), [(i, i ^ 5) for i in range(8)])
    near = jnp.stack([own, from_wide, from_narrow, from_both])
    across = lax.ppermute(near, "section", flip(2))
    core = lax.ppermute(near, "section", flip(1))
    far = lax.ppermute(across, "section", flip(1))
    return product_call((near, across, core, far), row_tiles)


def solution(mesh):
    in_specs = (
        P(None, "narrow", None),
        P(("section", "wide"), "narrow", None),
        P(),
        P(),
        P(),
        P(("section", "wide"), None),
        P(),
    )
    out_specs = P(("section", "narrow"), "wide")
    return jax.shard_map(on_device, mesh=mesh, in_specs=in_specs, out_specs=out_specs, check_vma=False)
```

```python
import functools
import math

import jax
import jax.numpy as jnp
import numpy as np
from jax import lax
from jax.experimental import pallas as pl
from jax.experimental.pallas import tpu as pltpu
from jax.sharding import PartitionSpec as P

LANES = 128
ROWS = 8
F32 = jnp.float32
BF16 = jnp.bfloat16


def cosine_table(length):
    wavenumber = np.arange(length, dtype=np.float64)[:, None]
    position = np.arange(length, dtype=np.float64)[None, :]
    table = math.sqrt(2.0 / length) * np.cos(
        math.pi * (2.0 * position + 1.0) * wavenumber / (2.0 * length)
    )
    table[0] *= math.sqrt(0.5)
    return table.astype(np.float32)


def split(value):
    high = value.astype(BF16)
    low = (value - high.astype(F32)).astype(BF16)
    return high, low


def z_weights(cosine, per_chunk, slot):
    extent = cosine.shape[0]
    out = np.zeros((per_chunk * extent, per_chunk * slot), np.float32)
    for y in range(per_chunk):
        out[y * extent : (y + 1) * extent, y * slot : y * slot + extent] = cosine.T
    return out


def y_weights(cosine):
    extent = cosine.shape[0]
    half = cosine[:, : extent // 2].reshape(extent * extent // 4, 2)
    return np.repeat(half, LANES // 2, axis=1)


def x_tables(cosine, planes, pairs):
    extent = cosine.shape[0]
    out = np.zeros((extent // planes, planes * pairs, LANES), np.float32)
    for part in range(extent // planes):
        block = cosine[:, part * planes : (part + 1) * planes].T
        out[part, :, :extent] = np.repeat(block, pairs, axis=0)
    return out


def pick_blocks(pairs, count, block_of, table_ref, out_ref, basis_ref, lane_ref, chunk_ref, first_ref):
    rows = table_ref.shape[1]
    per_plane = basis_ref.shape[0] // rows
    tiles = rows // ROWS
    scaled_ref = table_ref.at[per_plane]
    for s in range(per_plane):
        high, low = split(table_ref[s])
        basis_ref[pl.ds(s * rows, rows), pl.ds(0, LANES)] = high
        basis_ref[pl.ds(s * rows, rows), pl.ds(LANES, LANES)] = low
    index = table_ref[per_plane + 1 :].reshape(-1, LANES)[: lane_ref.shape[0]].astype(jnp.int32)
    lane_ref[...] = index & (LANES - 1)
    upper = index >> (LANES.bit_length() - 1)
    plane = (upper * ((1 << 16) // per_plane + 1)) >> 16
    first_ref[...] = plane
    chunk_ref[...] = upper - plane * per_plane
    take = functools.partial(jnp.take_along_axis, axis=1, mode="promise_in_bounds")
    wide = 2 * LANES
    inside = lax.broadcasted_iota(jnp.int32, (LANES, wide), 0).astype(F32).astype(BF16)
    one = jnp.ones((), BF16)
    zero = jnp.zeros((), BF16)

    def row_of(ref, b):
        return jnp.broadcast_to(ref[pl.ds(b, 1), :], (ROWS, LANES))

    def select(chunk, candidate):
        picked = [None] * tiles
        for c in range(per_plane):
            mine = chunk == c
            for t in range(tiles):
                found = candidate(c, t)
                picked[t] = found if c == 0 else jnp.where(mine, found, picked[t])
        return picked

    def finish(q, b, picked):
        first = row_of(first_ref, b)
        out = None
        for t in range(tiles):
            term = picked[t] * take(scaled_ref[pl.ds(t * ROWS, ROWS), :], first)
            out = term if out is None else out + term
        out = out + pltpu.roll(out, pairs, 0)
        out_ref[q] = out[:pairs]

    def three(step, carry):
        places = [step * 3 + u for u in range(3)]
        ids = [block_of(q) for q in places]
        lane = jnp.concatenate([lane_ref[pl.ds(b, 1), :] for b in ids[:2]], axis=1)
        hot = jnp.where(inside == lane.astype(F32).astype(BF16), one, zero)
        offers = jnp.dot(basis_ref[...], jnp.concatenate([hot, hot], axis=0), preferred_element_type=F32)
        third_lane = row_of(lane_ref, ids[2])
        third = select(row_of(chunk_ref, ids[2]), lambda c, t: take(table_ref[c, pl.ds(t * ROWS, ROWS), :], third_lane))
        chunk = jnp.concatenate([row_of(chunk_ref, b) for b in ids[:2]], axis=1)
        picked = select(chunk, lambda c, t: offers[c * rows + t * ROWS : c * rows + (t + 1) * ROWS])
        for u in range(2):
            finish(places[u], ids[u], [value[:, u * LANES : (u + 1) * LANES] for value in picked])
        finish(places[2], ids[2], third)
        return carry

    lax.fori_loop(0, count // 3, three, 0, unroll=16)


def sweep_kernel(
    sizes,
    *refs,
):
    given, (out_ref, table_ref), held = refs[:11], refs[11:13], refs[13:24]
    density_ref, fold_ref, *picking, sems = refs[24:]
    loads = [pltpu.make_async_copy(source, target, sems.at[i]) for i, (source, target) in enumerate(zip(given, held))]
    for load in loads[4:6] + loads[:4] + loads[6:]:
        load.start()
    bands_ref, valence_energy_ref, conduction_energy_ref, frequency_ref, *held = held
    valence_ref, conduction_ref, z_high_ref, z_low_ref, y_ref, x_ref, index_ref = held
    for load in loads[:4]:
        load.wait()
    loads = loads[4:]
    extent, planes, pairs, total_pairs, count, block_of = sizes
    rows = planes * pairs
    tiles = rows // ROWS
    per_tile = ROWS // pairs
    per_chunk = 3 * LANES // extent
    groups = extent // per_chunk
    row_id = lax.broadcasted_iota(jnp.int32, (ROWS, LANES), 0)
    lane_id = lax.broadcasted_iota(jnp.int32, (ROWS, LANES), 1)
    band = jnp.zeros((ROWS, LANES), jnp.int32)
    for p in range(pairs):
        band = jnp.where(row_id % pairs == p, bands_ref[0, p], band)
    loads[0].wait()
    loads[1].wait()
    for m in range(groups):
        for part in range(3):
            lanes = pl.ds((m * 3 + part) * LANES, LANES)
            for t in range(tiles):
                value, factor = None, None
                for u in range(per_tile):
                    plane = t * per_tile + u
                    picked = jnp.take_along_axis(valence_ref[plane, :, lanes], band, axis=0, mode="promise_in_bounds")
                    other = jnp.broadcast_to(conduction_ref[plane, :, lanes], (ROWS, LANES))
                    value = picked if u == 0 else jnp.where(row_id >= u * pairs, picked, value)
                    factor = other if u == 0 else jnp.where(row_id >= u * pairs, other, factor)
                density_ref[part, pl.ds(m * rows + t * ROWS, ROWS), :] = value * factor
    density = jnp.concatenate([density_ref[part] for part in range(3)], axis=1)
    high, low = split(density)
    loads[2].wait()
    loads[3].wait()
    dot = functools.partial(jnp.dot, preferred_element_type=F32)
    swept = dot(high, z_high_ref[...]) + dot(low, z_high_ref[...]) + dot(high, z_low_ref[...])
    quarter = per_chunk // 2
    for m in range(groups // 2):
        for q in range(quarter):
            near = swept[m * rows : (m + 1) * rows, q * LANES : (q + 1) * LANES]
            far_m, far_q = groups - 1 - m, quarter - 1 - q
            far = swept[far_m * rows : (far_m + 1) * rows, far_q * LANES : (far_q + 1) * LANES]
            far = pltpu.roll(far, LANES // 2, 1)
            fold_ref[0, m * quarter + q] = near + far
            fold_ref[1, m * quarter + q] = near - far
    terms = extent // 4
    block = 2 * ROWS
    loads[4].wait()

    def sweep_tiles(t, carry):
        where_rows = pl.ds(pl.multiple_of(t * block, block), block)
        for parity in range(2):
            parts = [fold_ref[parity, s, where_rows, :] for s in range(terms)]
            for j in range(parity, extent, 2):
                total = None
                for s in range(terms):
                    term = parts[s] * y_ref[pl.ds(j * terms + s, 1), :]
                    total = term if total is None else total + term
                total = total + pltpu.roll(total, LANES // 2, 1)
                start = j * extent
                offset = start % LANES
                moved = total if offset % (LANES // 2) == 0 else pltpu.roll(total, offset, 1)
                for chunk in range(start // LANES, (start + extent - 1) // LANES + 1):
                    low_lane = max(start - chunk * LANES, 0)
                    high_lane = min(start + extent - chunk * LANES, LANES)
                    table_ref[chunk, where_rows, low_lane:high_lane] = moved[:, low_lane:high_lane]
        return carry

    lax.fori_loop(0, rows // block, sweep_tiles, 0)
    per_plane = extent * extent // LANES
    loads[5].wait()
    loads[6].wait()
    narrow_pos = lax.axis_index("narrow")
    gap = jnp.zeros((ROWS, LANES), F32)
    for p in range(pairs):
        one_gap = conduction_energy_ref[bands_ref[1, p]] - valence_energy_ref[bands_ref[0, p]]
        gap = jnp.where(row_id % pairs == p, one_gap, gap)
    frequency = frequency_ref[0]
    scale = jnp.sqrt(4.0 * gap / (gap * gap + frequency * frequency) / math.sqrt(total_pairs))
    for t in range(tiles):
        table_ref[per_plane, pl.ds(t * ROWS, ROWS), :] = x_ref[narrow_pos, pl.ds(t * ROWS, ROWS), :] * scale
    blocks = index_ref.shape[0]
    for i in range(table_ref.shape[0] - per_plane - 1):
        some = min(rows, blocks - i * rows)
        table_ref[per_plane + 1 + i, pl.ds(0, some), :] = index_ref[pl.ds(i * rows, some), :].astype(F32)
    pick_blocks(pairs, count, block_of(), table_ref, out_ref, *picking)


def pick_kernel(pairs, count, block_of, *refs):
    pick_blocks(pairs, count, block_of(), *refs)


def pick_scratch(blocks, rows, area):
    return [pltpu.VMEM((area // LANES * rows, 2 * LANES), BF16)] + [pltpu.VMEM((blocks, LANES), jnp.int32)] * 3


VMEM = pl.BlockSpec(memory_space=pltpu.VMEM)
HBM = pl.BlockSpec(memory_space=pltpu.HBM)
ANY = pl.BlockSpec(memory_space=pl.ANY)


def sweep_call(bands, valence_energy, conduction_energy, frequency, valence, conduction, index, total_pairs, count, block_of):
    pairs = bands.shape[1]
    planes, area = valence.shape[0], valence.shape[2]
    extent = math.isqrt(area)
    rows = planes * pairs
    cosine = cosine_table(extent)
    per_chunk = 3 * LANES // extent
    groups = extent // per_chunk
    weights = z_weights(cosine, per_chunk, LANES // 2)
    z_high = weights.astype(BF16)
    z_low = (weights - z_high.astype(np.float32)).astype(BF16)
    operands = [valence, conduction, jnp.asarray(z_high), jnp.asarray(z_low)]
    operands += [jnp.asarray(y_weights(cosine)), jnp.asarray(x_tables(cosine, planes, pairs)), index]
    chunks = area // LANES
    blocks = index.shape[0]
    table = jax.ShapeDtypeStruct((area // LANES + 1 + -(-blocks // rows), rows, LANES), F32)
    scalars = [bands, valence_energy, conduction_energy, frequency]
    return pl.pallas_call(
        functools.partial(sweep_kernel, (extent, planes, pairs, total_pairs, count, block_of)),
        out_shape=[jax.ShapeDtypeStruct((count, pairs, LANES), F32), table],
        in_specs=[HBM] * 3 + [ANY] + [HBM] * len(operands),
        out_specs=[VMEM, VMEM],
        scratch_shapes=[pltpu.SMEM(a.shape, a.dtype) for a in scalars]
        + [pltpu.VMEM(a.shape, a.dtype) for a in operands]
        + [
            pltpu.VMEM((3, groups * rows, LANES), F32),
            pltpu.VMEM((2, extent // 4, rows, LANES), F32),
        ]
        + pick_scratch(blocks, rows, area)
        + [pltpu.SemaphoreType.DMA((len(scalars) + len(operands),))],
        compiler_params=pltpu.CompilerParams(vmem_limit_bytes=32 << 20),
        cost_estimate=pl.CostEstimate(flops=8_000_000_000, bytes_accessed=4_000_000, transcendentals=0),
        name="sweep",
    )(*(a if a is frequency else pltpu.with_memory_space_constraint(a, pltpu.HBM) for a in (*scalars, *operands)))


def pick_call(table, blocks, area, pairs, count, block_of):
    return pl.pallas_call(
        functools.partial(pick_kernel, pairs, count, block_of),
        out_shape=jax.ShapeDtypeStruct((count, pairs, LANES), F32),
        in_specs=[VMEM],
        out_specs=VMEM,
        scratch_shapes=pick_scratch(blocks, table.shape[1], area),
        compiler_params=pltpu.CompilerParams(vmem_limit_bytes=32 << 20),
        cost_estimate=pl.CostEstimate(flops=4_000_000_000, bytes_accessed=1_000_000, transcendentals=0),
        name="pick",
    )(table)


def arrange_kernel(row_tiles, near_ref, far_ref, own_ref, wide_ref, narrow_ref, both_ref):
    narrow_count = lax.axis_size("narrow")
    half = narrow_count * row_tiles
    wide_pos, narrow_pos = lax.axis_index("wide"), lax.axis_index("narrow")
    for out_ref, w, n in (
        (own_ref, wide_pos, narrow_pos),
        (wide_ref, 1 - wide_pos, narrow_pos),
        (narrow_ref, wide_pos, narrow_pos ^ 1),
        (both_ref, 1 - wide_pos, narrow_pos ^ 1),
    ):
        columns = pl.ds(w * half, half)
        rows = pl.ds((1 - w) * half + n * row_tiles, row_tiles)
        out_ref[pl.ds(0, half)] = near_ref[columns] + far_ref[columns]
        out_ref[pl.ds(half, row_tiles)] = near_ref[rows] + far_ref[rows]


def arrange_call(near, far, row_tiles):
    blocks, pairs, _ = near.shape
    shape = (blocks // 2 + row_tiles, pairs, LANES)
    return pl.pallas_call(
        functools.partial(arrange_kernel, row_tiles),
        out_shape=[jax.ShapeDtypeStruct(shape, F32)] * 4,
        in_specs=[VMEM] * 2,
        out_specs=[VMEM] * 4,
        compiler_params=pltpu.CompilerParams(vmem_limit_bytes=16 << 20),
        name="arrange",
    )(near, far)


def product_kernel(row_tiles, pairs, own_ref, across_ref, core_ref, far_ref, out_ref, rows_ref, gather_ref, value_ref, sems):
    section, wide_pos, narrow_pos = lax.axis_index("section"), lax.axis_index("wide"), lax.axis_index("narrow")
    parity = narrow_pos & 1
    narrow_count = lax.axis_size("narrow")
    half = narrow_count * row_tiles
    sources = (own_ref, across_ref, core_ref, far_ref)
    row_block = rows_ref.shape[0]

    piece = row_tiles // 2
    width = piece * LANES

    def collect(kind, start, count):
        for i, ref in enumerate(sources):
            for b in range(2):
                rows = pl.ds((2 * i + b) * pairs, pairs)
                for r in range(count):
                    gather_ref[rows, pl.ds(r * LANES, LANES)] = ref[2 * kind + b, start + r]
        return gather_ref[:, : count * LANES]

    start = jnp.where(section // 2 == wide_pos, narrow_pos * row_tiles, half)
    high, low = split(-collect((section & 1) ^ parity, start, row_tiles))
    high, low = high.astype(F32), low.astype(F32)
    rows_ref[...] = jnp.concatenate([high, high, low, low], axis=0).T.astype(BF16)

    def copy_of(step):
        columns = pl.ds(pl.multiple_of(step * width, width), width)
        return pltpu.make_async_copy(value_ref.at[:, columns], out_ref.at[:, columns], sems.at[step])

    def one_block(step, carry):
        per_kind = 2 * narrow_count
        high, low = split(collect((step // per_kind) ^ parity, (step % per_kind) * piece, piece))
        stacked = jnp.concatenate([high, low, high, low], axis=0)
        columns = pl.ds(pl.multiple_of(step * width, width), width)
        value_ref[:, columns] = jnp.dot(rows_ref[...], stacked, preferred_element_type=F32)
        copy_of(step).start()
        return carry

    def wait_block(step, carry):
        copy_of(step).wait()
        return carry

    steps = 4 * narrow_count
    lax.fori_loop(0, steps, one_block, 0)
    lax.fori_loop(0, steps, wait_block, 0)


def product_call(sources, row_tiles):
    _, blocks, pairs, _ = sources[0].shape
    row_block = row_tiles * LANES
    steps = 2 * (blocks // row_tiles - 1)
    depth = 2 * len(sources) * pairs
    return pl.pallas_call(
        functools.partial(product_kernel, row_tiles, pairs),
        out_shape=jax.ShapeDtypeStruct((row_block, steps * row_block), F32),
        in_specs=[VMEM] * len(sources),
        out_specs=pl.BlockSpec(memory_space=pl.ANY),
        scratch_shapes=[
            pltpu.VMEM((row_block, 4 * depth), BF16),
            pltpu.VMEM((depth, row_block), F32),
            pltpu.VMEM((row_block, steps * row_block), F32),
            pltpu.SemaphoreType.DMA((2 * steps,)),
        ],
        compiler_params=pltpu.CompilerParams(vmem_limit_bytes=40 << 20),
        name="product",
    )(*sources)


def contract(left_rows, right_rows):
    return lax.dot_general(
        left_rows,
        right_rows,
        (((0,), (0,)), ((), ())),
        precision=lax.Precision.HIGHEST,
        preferred_element_type=F32,
    )


def on_device(valence, conduction, valence_energy, conduction_energy, frequency, pair_bands, gvec_index):
    pairs = pair_bands.shape[0]
    section_count, wide_count, narrow_count = (lax.axis_size(name) for name in ("section", "wide", "narrow"))
    total_pairs = pairs * section_count * wide_count
    vector_count = gvec_index.shape[0]
    row_block = vector_count // (section_count * narrow_count)
    column_block = vector_count // wide_count
    row_tiles = row_block // LANES
    blocks = vector_count // LANES
    index = gvec_index.reshape(blocks, LANES)
    valence, conduction = (jnp.swapaxes(orbitals, 0, 1) for orbitals in (valence, conduction))
    energies = (valence_energy, conduction_energy, frequency)
    sweep = functools.partial(sweep_call, pair_bands.T, *energies, valence, conduction, index, total_pairs)

    if not (section_count == 4 and wide_count == 2 and narrow_count == 4):
        partial_value = sweep(blocks, lambda: lambda q: q)[0]
        partial_value = jnp.swapaxes(partial_value, 0, 1).reshape(pairs, section_count, narrow_count, row_block)
        own_rows = lax.psum_scatter(partial_value, "narrow", scatter_dimension=2, tiled=True)
        coefficients = lax.all_gather(own_rows, "narrow", axis=2, tiled=True).reshape(pairs, vector_count)
        row_send = own_rows.reshape(pairs, section_count, row_block)
        row_recv = lax.all_to_all(row_send, "section", split_axis=1, concat_axis=0, tiled=True)
        row_recv = row_recv.reshape(section_count, pairs, row_block)
        column_send = coefficients.reshape(pairs, wide_count, column_block)
        column_recv = lax.all_to_all(column_send, "wide", split_axis=1, concat_axis=0, tiled=True)
        column_recv = column_recv.reshape(wide_count * pairs, column_block)
        rows_all = lax.all_gather(row_recv, "wide", axis=1, tiled=True).reshape(-1, row_block)
        return contract(-rows_all, lax.all_gather(column_recv, "section", axis=0, tiled=True))

    half = narrow_count * row_tiles

    def block_of(other):
        def make():
            own = (lax.axis_index("narrow") & 1) ^ other
            return lambda q: q + (q // half + own) * half

        return make

    away, table = sweep(blocks // 2, block_of(1))
    kept = pick_call(table, blocks, valence.shape[2], pairs, blocks // 2, block_of(0))
    flip = lambda bit: [(i, i ^ bit) for i in range(4)]
    summed = kept + lax.ppermute(away, "narrow", flip(1))
    opposite = lax.ppermute(summed, "narrow", flip(2))
    own, to_wide, to_narrow, to_both = arrange_call(summed, opposite, row_tiles)
    from_wide = lax.ppermute(to_wide, "wide", [(0, 1), (1, 0)])
    from_narrow = lax.ppermute(to_narrow, "narrow", flip(1))
    from_both = lax.ppermute(to_both, ("wide", "narrow"), [(i, i ^ 5) for i in range(8)])
    near = jnp.stack([own, from_wide, from_narrow, from_both])
    across = lax.ppermute(near, "section", flip(2))
    core = lax.ppermute(near, "section", flip(1))
    far = lax.ppermute(across, "section", flip(1))
    return product_call((near, across, core, far), row_tiles)


def solution(mesh):
    in_specs = (
        P(None, "narrow", None),
        P(("section", "wide"), "narrow", None),
        P(),
        P(),
        P(),
        P(("section", "wide"), None),
        P(),
    )
    out_specs = P(("section", "narrow"), "wide")
    return jax.shard_map(on_device, mesh=mesh, in_specs=in_specs, out_specs=out_specs, check_vma=False)
```
